512 devices in a mesh: pair: 32 (over x_lo, z), virt: 16 (over y, x_hi, core).
Axes of the slice: x: 4 (x_hi: 2, x_lo: 2; x = x_hi * 2 + x_lo), y: 4, z: 16, core: 2. Of those that a mesh axis runs over, the one named last changes fastest.
Arguments:
- t_amps: bfloat16 [16384, 4096], P('pair', 'virt'), may hold values from -6 to 6
- v_ints: bfloat16 [16384, 4096], P('virt', 'pair'), may hold values from -0.09375 to 0.09375
- t_mask: int32 [128, 32], P('pair', 'virt'), may hold values 0 or 1
- v_mask: int32 [128, 32], P('virt'), may hold values from 0 to 1, as said below
Outputs:
- ladder: bfloat16 [16384, 16384], P('pair', 'virt')
The draws below stay inside these ranges and needn't reach their ends.
Inputs may be any that keep to these rules, and one draw needn't show every extreme that they name: `v_mask`: in each column and each aligned block of 8 rows (one device's ab tiles) between 1 and 4 entries are 1; in every column some block has exactly 4.
All inputs are finite; a program needn't handle non-finite values. No bound on the sum of `t_mask` on one device may be relied on, other than what follows from the above.
Results may differ from the reference program's by a relative error of at most 0.001.
Values may be sent and summed in bfloat16 or wider, within the bound.
No kernel may reach another device: no remote copies, remote signals or barrier semaphores. Data moves between devices by JAX's collectives and lax.ppermute only.
A program may use at most 64 MiB of HBM per device.

```python
import jax
import jax.numpy as jnp
from jax import lax

TILE = 128
PAIR_DEV = 512
NPAIR = 16384
AB = 16384
KCD = 4096
PT = 128
ABT = 128
KT = 32
ABT_DEV = 8
VCAP = 4
N_PAIR = 32
N_VIRT = 16


def draw_v_mask(key, part):
    base = jax.random.fold_in(key, 17)
    counts = jax.random.randint(jax.random.fold_in(base, 1), (N_VIRT, KT), 1, VCAP + 1)
    forced = jax.random.randint(jax.random.fold_in(base, 2), (KT,), 0, N_VIRT)
    rows_v = jnp.arange(N_VIRT, dtype=jnp.int32)[:, None]
    counts = jnp.where(rows_v == forced[None, :], VCAP, counts)
    keys = jax.random.split(jax.random.fold_in(base, 3), N_VIRT * KT)
    ranks = jax.vmap(lambda single: jax.random.permutation(single, ABT_DEV))(keys)
    ranks = ranks.reshape(N_VIRT, KT, ABT_DEV)
    ones = (ranks < counts[:, :, None]).astype(jnp.int32)
    return jnp.transpose(ones, (0, 2, 1)).reshape(ABT, KT)


def touch_ends(entries, rng, least, top_value):
    longest = entries.shape.index(max(entries.shape))
    spots = []
    for shift in (0, 1):
        where = [jax.random.randint(jax.random.fold_in(rng, axis), (), 0, length) for axis, length in enumerate(entries.shape)]
        where[longest] = (where[longest] + shift) % entries.shape[longest]
        spots.append(tuple(where))
    return entries.at[spots[0]].set(least).at[spots[1]].set(top_value)


def steps_of(key, extent, cuts, least, largest):
    def one(axis_at, shards_of):
        steps = jax.random.uniform(jax.random.fold_in(jax.random.fold_in(key, 6), axis_at), (shards_of,), jnp.float32, least / len(cuts), largest / len(cuts))
        return jnp.repeat(jnp.exp(steps), extent[axis_at] // shards_of).reshape((-1,) + (1,) * (len(extent) - axis_at - 1))

    level = one(*cuts[0])
    for cut in cuts[1:]:
        level = level * one(*cut)
    return level


def gaussian(own_key, shape, spread, limit, cuts=(), kind=jnp.bfloat16):
    loudness = steps_of(own_key, shape, cuts, -0.22, 0.18) if cuts else 1.0
    array = jax.random.normal(own_key, shape, jnp.float32) * spread * loudness
    return jnp.minimum(jnp.maximum(array, -limit), limit).astype(kind)


def setup_inputs(seed: int = 0) -> dict:
    arg_keys = jax.random.split(jax.random.key(seed), 5)
    return {
        "t_amps": gaussian(arg_keys[0], (NPAIR, KCD), 1.0, 6.0, ((0, 32), (1, 16))),
        "v_ints": gaussian(arg_keys[1], (AB, KCD), KCD ** -0.5, 0.09375, ((0, 16), (1, 32))),
        "t_mask": touch_ends((jax.random.randint(arg_keys[2], (PT, KT), 0, 4) < 3).astype(jnp.int32), jax.random.fold_in(arg_keys[2], 1), 0, 1),
        "v_mask": draw_v_mask(jax.random.fold_in(arg_keys[4], 71), 0),
    }


def expand(mask):
    return jnp.repeat(jnp.repeat(mask, TILE, axis=0), TILE, axis=1).astype(jnp.bfloat16)


def reference(t_amps, v_ints, t_mask, v_mask):
    masked_t = t_amps * expand(t_mask)
    masked_v = v_ints * expand(v_mask)
    blocks = masked_t.reshape(N_PAIR, PAIR_DEV, KCD)

    def one_block(rows):
        return lax.dot_general(rows, masked_v, (((1,), (1,)), ((), ())), preferred_element_type=jnp.float32).astype(jnp.bfloat16)

    return lax.map(one_block, blocks).reshape(NPAIR, AB)
```

```python
import jax
import jax.numpy as jnp
from jax import lax
from jax.experimental import pallas as pl
from jax.experimental.pallas import tpu as pltpu
from jax.sharding import PartitionSpec as P

TILE = 128
ABT_DEV = 8
VCAP = 4
NX, NZ, NY, NH = 2, 16, 4, 2
BOTH = ("pair", "virt")
CHUNK = VCAP * TILE


def moved(to):
    pairs = []
    for xl in range(NX):
        for z in range(NZ):
            for y in range(NY):
                for xh in range(NH):
                    for c in range(2):
                        a, b, d, e, g = to(xl, z, y, xh, c)
                        source = (xl * NZ + z) * 16 + y * 4 + xh * 2 + c
                        pairs.append((source, (a * NZ + b % NZ) * 16 + d * 4 + e * 2 + g))
    return pairs


RING = moved(lambda xl, z, y, xh, c: (xl, z + 1 - 2 * c, y, xh, c))
CORE = moved(lambda xl, z, y, xh, c: (xl, z, y, xh, 1 - c))
SIDE = moved(lambda xl, z, y, xh, c: (1 - xl, z, y, xh, c))
SAME_CORE = [[y * 4 + xh * 2 + c for y in range(NY) for xh in range(NH)] for c in range(2)]


def shift(x, pairs):
    return lax.ppermute(x, BOTH, pairs)


def pack_v_kernel(mask_ref, v_ref, out_ref):
    column = lax.axis_index("pair")
    flags = [mask_ref[a, column] for a in range(ABT_DEV)]
    chosen = sum(flags)
    taken = jnp.int32(0)
    for a in range(ABT_DEV):
        slot = jnp.where(flags[a] > 0, taken, chosen + a - taken)
        taken = taken + flags[a]

        @pl.when(slot < VCAP)
        def _():
            tile = v_ref[pl.ds(a * TILE, TILE), :] * flags[a].astype(jnp.bfloat16)
            out_ref[pl.ds(pl.multiple_of(slot * TILE, TILE), TILE), :] = tile.T


def pack_v(v_ints, v_mask):
    return pl.pallas_call(
        pack_v_kernel,
        out_shape=jax.ShapeDtypeStruct((CHUNK, TILE), jnp.bfloat16),
        in_specs=[
            pl.BlockSpec(memory_space=pltpu.SMEM),
            pl.BlockSpec(memory_space=pltpu.VMEM),
        ],
        out_specs=pl.BlockSpec(memory_space=pltpu.VMEM),
        name="pack_v",
    )(v_mask, v_ints)


def mask_t_kernel(mask_ref, t_ref, out_ref):
    for p in range(4):
        for k in range(2):
            at = (pl.ds(p * TILE, TILE), pl.ds(k * TILE, TILE))
            out_ref[(0, *at)] = t_ref[at] * mask_ref[p, k].astype(jnp.bfloat16)


def mask_t(t_amps, t_mask, copies):
    rows, cols = t_amps.shape
    return pl.pallas_call(
        mask_t_kernel,
        grid=(copies,),
        out_shape=jax.ShapeDtypeStruct((copies, rows, cols), jnp.bfloat16),
        in_specs=[
            pl.BlockSpec(memory_space=pltpu.SMEM),
            pl.BlockSpec((rows, cols), lambda i: (0, 0)),
        ],
        out_specs=pl.BlockSpec((1, rows, cols), lambda i: (i, 0, 0)),
        name="mask_t",
    )(t_mask, t_amps)


def slots_of(v_mask):
    rows = [v_mask[a] for a in range(ABT_DEV)]
    chosen = sum(rows)
    taken = jnp.zeros_like(chosen)
    slots = [jnp.zeros_like(chosen) for _ in range(VCAP)]
    for a in range(ABT_DEV):
        slot = jnp.where(rows[a] > 0, taken, chosen + a - taken)
        taken = taken + rows[a]
        slots = [s + jnp.where(slot == j, a, 0) for j, s in enumerate(slots)]
    return jnp.stack(slots)


def product_kernel(plan, last, slot_ref, own_ref, other_ref, *refs):
    n = len(plan)
    chunks, refs = refs[:n], refs[n:]
    before = None
    if len(refs) == 4:
        before, refs = refs[0], refs[1:]
    out_ref, left, right = refs
    pair, virt = lax.axis_index("pair"), lax.axis_index("virt")
    xl, z, core = pair // NZ, pair % NZ, virt % 2
    way = 1 - 2 * core
    right[...] = jnp.zeros_like(right)
    for i, (across, step) in enumerate(plan):
        depth = lax.rem(z + step * way + NZ, NZ)
        k = (xl if not across else 1 - xl) * NZ + depth
        member = k // 4
        half = pl.multiple_of((k % 2) * TILE, TILE)
        mine = ((k // 2) % 2) == core
        at = pl.ds(i * TILE, TILE)
        left[:, at] = jnp.where(
            mine, own_ref[member, :, pl.ds(half, TILE)], other_ref[member, :, pl.ds(half, TILE)]
        )
        for j in range(VCAP):
            to = pl.multiple_of(slot_ref[j, k] * TILE, TILE)
            right[at, pl.ds(to, TILE)] = chunks[i][pl.ds(j * TILE, TILE), :]

    def columns(i, _):
        at = pl.ds(pl.multiple_of(i * 256, 256), 256)
        total = jnp.dot(left[...], right[:, at], preferred_element_type=jnp.float32)
        if before is not None:
            total = total + before[:, at]
        out_ref[:, at] = total.astype(out_ref.dtype)
        return 0

    lax.fori_loop(0, out_ref.shape[1] // 256, columns, 0)


def product(slots, t_own, t_other, chunks, before, last, name):
    rows, cols = t_own.shape[1], ABT_DEV * TILE
    plan = tuple((across, step) for _, _, across, step in chunks)
    depth = len(plan) * TILE

    def kernel(*refs):
        product_kernel(plan, last, *refs)

    whole = pl.BlockSpec(memory_space=pltpu.VMEM)
    specs = [pl.BlockSpec(memory_space=pltpu.SMEM), whole, whole]
    args = [slots, t_own, t_other]
    for array, block, _, _ in chunks:
        args.append(array)
        specs.append(pl.BlockSpec((CHUNK, TILE), lambda i, block=block: (block, 0)))
    if before is not None:
        args.append(before)
        specs.append(whole)
    return pl.pallas_call(
        kernel,
        grid=(1,),
        out_shape=jax.ShapeDtypeStruct((rows, cols), jnp.bfloat16 if last else jnp.float32),
        in_specs=specs,
        out_specs=whole,
        scratch_shapes=[
            pltpu.VMEM((rows, depth), jnp.bfloat16),
            pltpu.VMEM((depth, cols), jnp.bfloat16),
        ],
        compiler_params=pltpu.CompilerParams(vmem_limit_bytes=32 * 1024 * 1024),
        cost_estimate=pl.CostEstimate(
            flops=2 * rows * depth * cols,
            bytes_accessed=4 * rows * cols + 2 * depth * TILE * 4,
            transcendentals=0,
        ),
        name=name,
    )(*args)


def local(t_amps, v_ints, t_mask, v_mask):
    own = pack_v(v_ints, v_mask)
    own_c = shift(own, CORE)
    side = shift(own, SIDE)
    a = [jnp.concatenate([own, own_c])]
    spread = mask_t(t_amps, t_mask, len(SAME_CORE[0]))
    t_own = lax.all_to_all(spread, "virt", 0, 0, axis_index_groups=SAME_CORE, tiled=True)
    side_c = shift(side, CORE)
    b = [jnp.concatenate([side, side_c])]
    for _ in range(7):
        a.append(shift(a[-1], RING))
        b.append(shift(b[-1], RING))
    a8 = shift(a[7][:CHUNK], RING)
    b8 = shift(b[7][:CHUNK], RING)
    t_other = shift(t_own, CORE)
    slots = slots_of(v_mask)
    near = jnp.concatenate([w[s][CHUNK:] for s in range(1, 5) for w in (a, b)])
    near = shift(near, CORE)
    far = jnp.concatenate([w[s][CHUNK:] for s in range(5, 8) for w in (a, b)])
    far = shift(far, CORE)
    first = [(own, 0, False, 0), (side, 0, True, 0)]
    for s in range(1, 5):
        first += [(a[s], 0, False, -s), (b[s], 0, True, -s)]
        first += [(near, 2 * (s - 1), False, s), (near, 2 * (s - 1) + 1, True, s)]
    second = []
    for s in range(5, 8):
        second += [(a[s], 0, False, -s), (b[s], 0, True, -s)]
    third = [(a8, 0, False, -8), (b8, 0, True, -8)]
    for s in range(5, 8):
        third += [(far, 2 * (s - 5), False, s), (far, 2 * (s - 5) + 1, True, s)]
    total = product(slots, t_own, t_other, first, None, False, "first")
    total = product(slots, t_own, t_other, second, total, False, "second")
    return product(slots, t_own, t_other, third, total, True, "third")


def solution(mesh):
    return jax.shard_map(
        local,
        mesh=mesh,
        in_specs=(P("pair", "virt"), P("virt", "pair"), P("pair", "virt"), P("virt", None)),
        out_specs=P("pair", "virt"),
        check_vma=False,
    )
```

```python
import functools

import jax
import jax.numpy as jnp
from jax import lax
from jax.experimental import pallas as pl
from jax.experimental.pallas import tpu as pltpu
from jax.sharding import PartitionSpec as P


TILE = 128
ABT_DEV = 8
VCAP = 4
NX, NZ, NY, NH = 2, 16, 4, 2
BOTH = ("pair", "virt")
CHUNK = VCAP * TILE


def moved(to):
    pairs = []
    for xl in range(NX):
        for z in range(NZ):
            for y in range(NY):
                for xh in range(NH):
                    for c in range(2):
                        a, b, d, e, g = to(xl, z, y, xh, c)
                        source = (xl * NZ + z) * 16 + y * 4 + xh * 2 + c
                        pairs.append((source, (a * NZ + b % NZ) * 16 + d * 4 + e * 2 + g))
    return pairs


STILL, MINE, OTHER = 0, 1, 2
RING1 = moved(lambda xl, z, y, xh, c: (xl, z + 1 - 2 * c, y, xh, c))
RING2 = moved(lambda xl, z, y, xh, c: (xl, z + 2 - 4 * c, y, xh, c))
CORE = moved(lambda xl, z, y, xh, c: (xl, z, y, xh, 1 - c))
SIDE = moved(lambda xl, z, y, xh, c: (1 - xl, z, y, xh, c))
SAME_CORE = [[y * 4 + xh * 2 + c for y in range(NY) for xh in range(NH)] for c in range(2)]
CORES = [[y * 4 + xh * 2 + c for c in range(2)] for y in range(NY) for xh in range(NH)]


def limit(mib):
    return pltpu.CompilerParams(vmem_limit_bytes=mib * 1024 * 1024)


def shift(x, pairs):
    return lax.ppermute(x, BOTH, pairs)


def pack_v_kernel(mask_ref, v_ref, out_ref):
    column = lax.axis_index("pair")
    flags = [mask_ref[a, column] for a in range(ABT_DEV)]
    chosen = sum(flags)
    taken = jnp.int32(0)
    for a in range(ABT_DEV):
        slot = jnp.where(flags[a] > 0, taken, chosen + a - taken)
        taken = taken + flags[a]

        @pl.when(slot < VCAP)
        def _():
            tile = v_ref[pl.ds(a * TILE, TILE), :] * flags[a].astype(jnp.bfloat16)
            out_ref[pl.ds(pl.multiple_of(slot * TILE, TILE), TILE), :] = tile.T


def pack_v(v_ints, v_mask):
    return pl.pallas_call(
        pack_v_kernel,
        grid=(1,),
        out_shape=jax.ShapeDtypeStruct((CHUNK, TILE), jnp.bfloat16),
        in_specs=[
            pl.BlockSpec(memory_space=pltpu.SMEM),
            pl.BlockSpec(v_ints.shape, lambda i: (0, 0)),
        ],
        out_specs=pl.BlockSpec(memory_space=pltpu.VMEM),
        compiler_params=limit(4),
        name="pack_v",
    )(v_mask, v_ints)


def mask_t_kernel(mask_ref, t_ref, out_ref):
    for p in range(4):
        for k in range(2):
            at = (pl.ds(p * TILE, TILE), pl.ds(k * TILE, TILE))
            tile = t_ref[at] * mask_ref[k, p].astype(jnp.bfloat16)
            for i in range(out_ref.shape[0]):
                out_ref[(i, *at)] = tile


def mask_t(t_amps, t_mask, copies):
    rows, cols = t_amps.shape
    return pl.pallas_call(
        mask_t_kernel,
        grid=(1,),
        out_shape=jax.ShapeDtypeStruct((copies, rows, cols), jnp.bfloat16),
        in_specs=[
            pl.BlockSpec(memory_space=pltpu.SMEM),
            pl.BlockSpec((rows, cols), lambda i: (0, 0)),
        ],
        out_specs=pl.BlockSpec((copies, rows, cols), lambda i: (0, 0, 0)),
        compiler_params=limit(6),
        name="mask_t",
    )(t_mask.T, t_amps)


def collect_kernel(pieces, count, *refs):
    core = lax.axis_index("virt") % 2
    to = 0
    for array, base, rows, side in pieces:
        refs[count][pl.ds(to, rows), :] = refs[array][pl.ds(start(base, side, core), rows), :]
        to += rows


def start(base, side, core):
    if side == STILL:
        return base
    return pl.multiple_of(base + (core if side == MINE else 1 - core) * CHUNK, CHUNK)


def indexed(pieces):
    arrays, where = [], []
    for array, *rest in pieces:
        at = next((i for i, seen in enumerate(arrays) if seen is array), len(arrays))
        if at == len(arrays):
            arrays.append(array)
        where.append((at, *rest))
    return arrays, where


def collect(*pieces):
    arrays, where = indexed(pieces)
    whole = pl.BlockSpec(memory_space=pltpu.VMEM)
    return pl.pallas_call(
        functools.partial(collect_kernel, where, len(arrays)),
        out_shape=jax.ShapeDtypeStruct((sum(p[2] for p in where), TILE), jnp.bfloat16),
        in_specs=[whole] * len(arrays),
        out_specs=whole,
        compiler_params=limit(4),
        name="collect",
    )(*arrays)


def slots_of(v_mask):
    rows = [v_mask[a] for a in range(ABT_DEV)]
    chosen = sum(rows)
    taken = jnp.zeros_like(chosen)
    slots = [jnp.zeros_like(chosen) for _ in range(VCAP)]
    for a in range(ABT_DEV):
        slot = jnp.where(rows[a] > 0, taken, chosen + a - taken)
        taken = taken + rows[a]
        slots = [s + jnp.where(slot == j, a, 0) for j, s in enumerate(slots)]
    return jnp.stack(slots)


def product_kernel(plan, count, adds, slot_ref, own_ref, other_ref, *refs):
    arrays, refs = refs[:count], refs[count:]
    before = None
    if adds:
        before, refs = refs[0], refs[1:]
    out_ref, left, right = refs
    pair, virt = lax.axis_index("pair"), lax.axis_index("virt")
    xl, z, core = pair // NZ, pair % NZ, virt % 2
    way = 1 - 2 * core
    right[...] = jnp.zeros_like(right)
    for i, (array, base, side, across, step) in enumerate(plan):
        depth = lax.rem(z + step * way + NZ, NZ)
        k = (xl if not across else 1 - xl) * NZ + depth
        member = k // 4
        half = pl.multiple_of((k % 2) * TILE, TILE)
        mine = ((k // 2) % 2) == core
        at = pl.ds(i * TILE, TILE)
        left[:, at] = jnp.where(
            mine, own_ref[member, :, pl.ds(half, TILE)], other_ref[member, :, pl.ds(half, TILE)]
        )
        first = start(base, side, core)
        for j in range(VCAP):
            to = pl.multiple_of(slot_ref[j, k] * TILE, TILE)
            right[at, pl.ds(to, TILE)] = arrays[array][pl.ds(first + j * TILE, TILE), :]

    def columns(i, _):
        at = pl.ds(pl.multiple_of(i * 256, 256), 256)
        total = jnp.dot(left[...], right[:, at], preferred_element_type=jnp.float32)
        if before is not None:
            total = total + before[:, at]
        out_ref[:, at] = total.astype(out_ref.dtype)
        return 0

    lax.fori_loop(0, out_ref.shape[1] // 256, columns, 0)


def product(slots, t_own, t_other, chunks, before, last):
    rows, cols = t_own.shape[1], ABT_DEV * TILE
    arrays, plan = indexed(chunks)
    depth = len(plan) * TILE

    def kernel(*refs):
        product_kernel(plan, len(arrays), before is not None, *refs)

    whole = pl.BlockSpec(memory_space=pltpu.VMEM)
    args = [slots, t_own, t_other, *arrays] + ([] if before is None else [before])
    return pl.pallas_call(
        kernel,
        out_shape=jax.ShapeDtypeStruct((rows, cols), jnp.bfloat16 if last else jnp.float32),
        in_specs=[pl.BlockSpec(memory_space=pltpu.SMEM)] + [whole] * (len(args) - 1),
        out_specs=whole,
        scratch_shapes=[
            pltpu.VMEM((rows, depth), jnp.bfloat16),
            pltpu.VMEM((depth, cols), jnp.bfloat16),
        ],
        compiler_params=limit(14),
        cost_estimate=pl.CostEstimate(
            flops=2 * rows * depth * cols,
            bytes_accessed=4 * rows * cols + 2 * depth * TILE * 4,
            transcendentals=0,
        ),
    )(*args)


def both_cores(x):
    return lax.all_gather(x, "virt", axis=0, axis_index_groups=CORES, tiled=True)


def ladder(t_amps, v_ints, t_mask, v_mask):
    own = pack_v(v_ints, v_mask)
    side = shift(own, SIDE)
    both = both_cores(own)
    d = {}
    for s in range(1, 8):
        d[s] = shift(both, RING1) if s == 1 else shift(d[s - 2] if s > 2 else both, RING2)
    d8 = collect((d[6], 0, CHUNK, MINE))
    d8 = shift(d8, RING2)
    spread = mask_t(t_amps, t_mask, len(SAME_CORE[0]))
    t_own = lax.all_to_all(spread, "virt", 0, 0, axis_index_groups=SAME_CORE, tiled=True)
    t_other = shift(t_own, CORE)
    slots = slots_of(v_mask)
    x = {}
    for i in (1, 2, 3):
        x[i] = collect((d[2 * i - 1], 0, 2 * CHUNK, STILL), (d[2 * i], 0, 2 * CHUNK, STILL))
        x[i] = shift(x[i], SIDE)
    x[4] = collect((d[7], 0, 2 * CHUNK, STILL), (d8, 0, CHUNK, STILL))
    x[4] = shift(x[4], SIDE)

    def blocks(steps):
        for s in steps:
            yield s, False, d[s], 0
            yield s, True, x[(s + 1) // 2], (s + 1) % 2 * 2 * CHUNK

    def exchange(steps):
        rest = collect(*((array, base, CHUNK, OTHER) for _, _, array, base in blocks(steps)))
        return shift(rest, CORE)

    def direct(steps):
        return [(array, base, MINE, across, -s) for s, across, array, base in blocks(steps)]

    def exchanged(rest, steps):
        return [
            (rest, i * CHUNK, STILL, across, s) for i, (s, across, _, _) in enumerate(blocks(steps))
        ]

    batches = {"near": (1, 2, 3, 4), "far": (5, 6), "end": (7,)}
    rest = {name: exchange(steps) for name, steps in batches.items()}
    first = [(own, 0, STILL, False, 0), (side, 0, STILL, True, 0)]
    first += direct(batches["near"]) + exchanged(rest["near"], batches["near"])
    second = direct(batches["far"]) + exchanged(rest["far"], batches["far"]) + direct(batches["end"])
    second += [(d8, 0, STILL, False, -8), (x[4], 2 * CHUNK, STILL, True, -8)]
    third = exchanged(rest["end"], batches["end"])
    total = product(slots, t_own, t_other, first, None, False)
    total = product(slots, t_own, t_other, second, total, False)
    return product(slots, t_own, t_other, third, total, True)


def solution(mesh):
    return jax.shard_map(
        ladder,
        mesh=mesh,
        in_specs=(P("pair", "virt"), P("virt", "pair"), P("pair", "virt"), P("virt", None)),
        out_specs=P("pair", "virt"),
        check_vma=False,
    )
```

```python
import functools

import jax
import jax.numpy as jnp
from jax import lax
from jax.experimental import pallas as pl
from jax.experimental.pallas import tpu as pltpu
from jax.sharding import PartitionSpec as P


TILE = 128
ABT_DEV = 8
VCAP = 4
NX, NZ, NY, NH = 2, 16, 4, 2
BOTH = ("pair", "virt")
CHUNK = VCAP * TILE


def moved(to):
    pairs = []
    for xl in range(NX):
        for z in range(NZ):
            for y in range(NY):
                for xh in range(NH):
                    for c in range(2):
                        a, b, d, e, g = to(xl, z, y, xh, c)
                        source = (xl * NZ + z) * 16 + y * 4 + xh * 2 + c
                        pairs.append((source, (a * NZ + b % NZ) * 16 + d * 4 + e * 2 + g))
    return pairs


STILL, MINE, OTHER = 0, 1, 2
RING = moved(lambda xl, z, y, xh, c: (xl, z + 1 - 2 * c, y, xh, c))
LEAP = moved(lambda xl, z, y, xh, c: (xl, z + 5 - 10 * c, y, xh, c))
CORE = moved(lambda xl, z, y, xh, c: (xl, z, y, xh, 1 - c))
SIDE = moved(lambda xl, z, y, xh, c: (1 - xl, z, y, xh, c))
SAME_CORE = [[y * 4 + xh * 2 + c for y in range(NY) for xh in range(NH)] for c in range(2)]
CORES = [[y * 4 + xh * 2 + c for c in range(2)] for y in range(NY) for xh in range(NH)]


def limit(mib):
    return pltpu.CompilerParams(vmem_limit_bytes=mib * 1024 * 1024)


def shift(x, pairs):
    return lax.ppermute(x, BOTH, pairs)


def pack_kernel(v_mask_ref, t_mask_ref, v_ref, t_ref, v_out, t_out):
    column = lax.axis_index("pair")
    flags = [v_mask_ref[a, column] for a in range(ABT_DEV)]
    chosen = sum(flags)
    taken = jnp.int32(0)
    for a in range(ABT_DEV):
        slot = jnp.where(flags[a] > 0, taken, chosen + a - taken)
        taken = taken + flags[a]

        @pl.when(slot < VCAP)
        def _():
            tile = v_ref[pl.ds(a * TILE, TILE), :] * flags[a].astype(jnp.bfloat16)
            v_out[pl.ds(pl.multiple_of(slot * TILE, TILE), TILE), :] = tile.T

    for p in range(t_mask_ref.shape[1]):
        for k in range(t_mask_ref.shape[0]):
            at = (pl.ds(p * TILE, TILE), pl.ds(k * TILE, TILE))
            t_out[at] = t_ref[at] * t_mask_ref[k, p].astype(jnp.bfloat16)


def pack(v_ints, t_amps, v_mask, t_mask):
    def block(shape):
        return pl.BlockSpec(shape, lambda i: (0, 0))

    return pl.pallas_call(
        pack_kernel,
        grid=(1,),
        out_shape=[
            jax.ShapeDtypeStruct((CHUNK, TILE), jnp.bfloat16),
            jax.ShapeDtypeStruct(t_amps.shape, jnp.bfloat16),
        ],
        in_specs=[
            pl.BlockSpec(memory_space=pltpu.SMEM),
            pl.BlockSpec(memory_space=pltpu.SMEM),
            block(v_ints.shape),
            block(t_amps.shape),
        ],
        out_specs=[block((CHUNK, TILE)), block(t_amps.shape)],
        name="pack",
    )(v_mask, t_mask.T, v_ints, t_amps)


def collect_kernel(pieces, count, *refs):
    core = lax.axis_index("virt") % 2
    to = 0
    for array, base, rows, side in pieces:
        refs[count][pl.ds(to, rows), :] = refs[array][pl.ds(start(base, side, core), rows), :]
        to += rows


def start(base, side, core):
    if side == STILL:
        return base
    return pl.multiple_of(base + (core if side == MINE else 1 - core) * CHUNK, CHUNK)


def indexed(pieces):
    arrays, where = [], []
    for array, *rest in pieces:
        at = next((i for i, seen in enumerate(arrays) if seen is array), len(arrays))
        if at == len(arrays):
            arrays.append(array)
        where.append((at, *rest))
    return arrays, where


def collect(*pieces):
    arrays, where = indexed(pieces)
    whole = pl.BlockSpec(memory_space=pltpu.VMEM)
    return pl.pallas_call(
        functools.partial(collect_kernel, where, len(arrays)),
        out_shape=jax.ShapeDtypeStruct((sum(p[2] for p in where), TILE), jnp.bfloat16),
        in_specs=[whole] * len(arrays),
        out_specs=whole,
        compiler_params=limit(4),
        name="collect",
    )(*arrays)


def slots_of(v_mask):
    rows = [v_mask[a] for a in range(ABT_DEV)]
    chosen = sum(rows)
    taken = jnp.zeros_like(chosen)
    slots = [jnp.zeros_like(chosen) for _ in range(VCAP)]
    for a in range(ABT_DEV):
        slot = jnp.where(rows[a] > 0, taken, chosen + a - taken)
        taken = taken + rows[a]
        slots = [s + jnp.where(slot == j, a, 0) for j, s in enumerate(slots)]
    return jnp.stack(slots)


def product_kernel(plan, count, adds, slot_ref, own_ref, other_ref, *refs):
    arrays, refs = refs[:count], refs[count:]
    before = None
    if adds:
        before, refs = refs[0], refs[1:]
    out_ref, left, right = refs
    pair, virt = lax.axis_index("pair"), lax.axis_index("virt")
    xl, z, core = pair // NZ, pair % NZ, virt % 2
    way = 1 - 2 * core
    right[...] = jnp.zeros_like(right)
    for i, (array, base, side, across, step) in enumerate(plan):
        depth = lax.rem(z + step * way + NZ, NZ)
        k = (xl if not across else 1 - xl) * NZ + depth
        member = k // 4
        half = pl.multiple_of((k % 2) * TILE, TILE)
        mine = ((k // 2) % 2) == core
        at = pl.ds(i * TILE, TILE)
        left[:, at] = jnp.where(
            mine, own_ref[member, :, pl.ds(half, TILE)], other_ref[member, :, pl.ds(half, TILE)]
        )
        first = start(base, side, core)
        for j in range(VCAP):
            to = pl.multiple_of(slot_ref[j, k] * TILE, TILE)
            right[at, pl.ds(to, TILE)] = arrays[array][pl.ds(first + j * TILE, TILE), :]

    def columns(i, _):
        at = pl.ds(pl.multiple_of(i * 256, 256), 256)
        total = jnp.dot(left[...], right[:, at], preferred_element_type=jnp.float32)
        if before is not None:
            total = total + before[:, at]
        out_ref[:, at] = total.astype(out_ref.dtype)
        return 0

    lax.fori_loop(0, out_ref.shape[1] // 256, columns, 0)


def product(slots, t_own, t_other, chunks, before, last):
    rows, cols = t_own.shape[1], ABT_DEV * TILE
    arrays, plan = indexed(chunks)
    depth = len(plan) * TILE

    def kernel(*refs):
        product_kernel(plan, len(arrays), before is not None, *refs)

    whole = pl.BlockSpec(memory_space=pltpu.VMEM)
    args = [slots, t_own, t_other, *arrays] + ([] if before is None else [before])
    return pl.pallas_call(
        kernel,
        out_shape=jax.ShapeDtypeStruct((rows, cols), jnp.bfloat16 if last else jnp.float32),
        in_specs=[pl.BlockSpec(memory_space=pltpu.SMEM)] + [whole] * (len(args) - 1),
        out_specs=whole,
        scratch_shapes=[
            pltpu.VMEM((rows, depth), jnp.bfloat16),
            pltpu.VMEM((depth, cols), jnp.bfloat16),
        ],
        compiler_params=limit(14),
        cost_estimate=pl.CostEstimate(
            flops=2 * rows * depth * cols,
            bytes_accessed=4 * rows * cols + 2 * depth * TILE * 4,
            transcendentals=0,
        ),
    )(*args)


def both_cores(x):
    return lax.all_gather(x, "virt", axis=0, axis_index_groups=CORES, tiled=True)


def ladder(t_amps, v_ints, t_mask, v_mask):
    own, t_masked = pack(v_ints, t_amps, v_mask, t_mask)
    side = shift(own, SIDE)
    d = {0: both_cores(own)}
    for s in range(1, 8):
        d[s] = shift(d[s - 1], RING)
    d8 = collect((d[3], 0, CHUNK, MINE))
    d8 = shift(d8, LEAP)
    t_masked = jnp.broadcast_to(t_masked, (len(SAME_CORE[0]), *t_masked.shape))
    t_own = lax.all_to_all(t_masked, "virt", 0, 0, axis_index_groups=SAME_CORE, tiled=True)
    t_other = shift(t_own, CORE)
    slots = slots_of(v_mask)

    x = {}
    for parts in FORWARD.values():
        arrays = [(d8, 0, CHUNK, STILL) if s == 8 else (d[s], 0, 2 * CHUNK, STILL) for s in parts]
        packed = arrays[0][0]
        if len(arrays) > 1:
            packed = collect(*arrays)
        packed = shift(packed, SIDE)
        for i, s in enumerate(parts):
            x[s] = (packed, 2 * CHUNK * i)

    def exchange(columns):
        sources = [(x[s] if across else (d[s], 0)) for s, across in columns]
        rest = collect(*((array, base, CHUNK, OTHER) for array, base in sources))
        rest = shift(rest, CORE)
        return [(rest, i * CHUNK, STILL, across, s) for i, (s, across) in enumerate(columns)]

    def direct(*columns):
        return [
            (*(x[s] if across else (d[s], 0)), MINE, across, -s) for s, across in columns
        ]

    near = exchange([(s, False) for s in range(1, 7)] + [(s, True) for s in range(1, 5)])
    end = exchange([(5, True), (6, True), (7, False), (7, True)])
    zero = [(own, 0, STILL, False, 0), (side, 0, STILL, True, 0)]
    zero += direct(*((s, False) for s in range(1, 5)), (1, True), (2, True))
    first = direct((5, False), (6, False), (3, True), (4, True)) + near
    second = direct((5, True), (6, True), (7, False), (7, True))
    second += [(d8, 0, STILL, False, -8), (*x[8], STILL, True, -8)]
    total = None
    for name, chunks in (("zero", zero), ("first", first), ("second", second), ("third", end)):
        total = product(slots, t_own, t_other, chunks, total, name == "third")
    return total


FORWARD = {"x12": (1, 2), "x34": (3, 4), "x5": (5,), "x68": (6, 8), "x7": (7,)}


def solution(mesh):
    return jax.shard_map(
        ladder,
        mesh=mesh,
        in_specs=(P("pair", "virt"), P("virt", "pair"), P("pair", "virt"), P("virt", None)),
        out_specs=P("pair", "virt"),
        check_vma=False,
    )
```

```python
import functools

import jax
import jax.numpy as jnp
from jax import lax
from jax.experimental import pallas as pl
from jax.experimental.pallas import tpu as pltpu
from jax.sharding import PartitionSpec as P


TILE = 128
ABT_DEV = 8
VCAP = 4
NX, NZ, NY, NH = 2, 16, 4, 2
BOTH = ("pair", "virt")
CHUNK = VCAP * TILE


def moved(to):
    pairs = []
    for xl in range(NX):
        for z in range(NZ):
            for y in range(NY):
                for xh in range(NH):
                    for c in range(2):
                        a, b, d, e, g = to(xl, z, y, xh, c)
                        source = (xl * NZ + z) * 16 + y * 4 + xh * 2 + c
                        pairs.append((source, (a * NZ + b % NZ) * 16 + d * 4 + e * 2 + g))
    return pairs


STILL, MINE, OTHER = 0, 1, 2
RING = moved(lambda xl, z, y, xh, c: (xl, z + 1 - 2 * c, y, xh, c))
LEAP = moved(lambda xl, z, y, xh, c: (xl, z + 7 - 14 * c, y, xh, c))
CORE = moved(lambda xl, z, y, xh, c: (xl, z, y, xh, 1 - c))
SIDE = moved(lambda xl, z, y, xh, c: (1 - xl, z, y, xh, c))
SAME_CORE = [[y * 4 + xh * 2 + c for y in range(NY) for xh in range(NH)] for c in range(2)]
CORES = [[y * 4 + xh * 2 + c for c in range(2)] for y in range(NY) for xh in range(NH)]


def limit(mib):
    return pltpu.CompilerParams(vmem_limit_bytes=mib * 1024 * 1024)


def shift(x, pairs):
    return lax.ppermute(x, BOTH, pairs)


def pack_kernel(v_mask_ref, t_mask_ref, v_ref, t_ref, v_out, t_out):
    column = lax.axis_index("pair")
    flags = [v_mask_ref[a, column] for a in range(ABT_DEV)]
    chosen = sum(flags)
    taken = jnp.int32(0)
    for a in range(ABT_DEV):
        slot = jnp.where(flags[a] > 0, taken, chosen + a - taken)
        taken = taken + flags[a]

        @pl.when(slot < VCAP)
        def _():
            tile = v_ref[pl.ds(a * TILE, TILE), :] * flags[a].astype(jnp.bfloat16)
            v_out[pl.ds(pl.multiple_of(slot * TILE, TILE), TILE), :] = tile.T

    for p in range(t_mask_ref.shape[1]):
        for k in range(t_mask_ref.shape[0]):
            at = (pl.ds(p * TILE, TILE), pl.ds(k * TILE, TILE))
            tile = t_ref[at] * t_mask_ref[k, p].astype(jnp.bfloat16)
            for i in range(t_out.shape[0]):
                t_out[(i, *at)] = tile


def pack(v_ints, t_amps, v_mask, t_mask, copies):
    spread = (copies, *t_amps.shape)

    def block(shape):
        return pl.BlockSpec(shape, lambda i: (0,) * len(shape))

    return pl.pallas_call(
        pack_kernel,
        grid=(1,),
        out_shape=[
            jax.ShapeDtypeStruct((CHUNK, TILE), jnp.bfloat16),
            jax.ShapeDtypeStruct(spread, jnp.bfloat16),
        ],
        in_specs=[
            pl.BlockSpec(memory_space=pltpu.SMEM),
            pl.BlockSpec(memory_space=pltpu.SMEM),
            block(v_ints.shape),
            block(t_amps.shape),
        ],
        out_specs=[block((CHUNK, TILE)), block(spread)],
        name="pack",
    )(v_mask, t_mask.T, v_ints, t_amps)


def collect_kernel(pieces, count, *refs):
    core = lax.axis_index("virt") % 2
    to = 0
    for array, base, rows, side in pieces:
        refs[count][pl.ds(to, rows), :] = refs[array][pl.ds(start(base, side, core), rows), :]
        to += rows


def start(base, side, core):
    if side == STILL:
        return base
    return pl.multiple_of(base + (core if side == MINE else 1 - core) * CHUNK, CHUNK)


def indexed(pieces):
    arrays, where = [], []
    for array, *rest in pieces:
        at = next((i for i, seen in enumerate(arrays) if seen is array), len(arrays))
        if at == len(arrays):
            arrays.append(array)
        where.append((at, *rest))
    return arrays, where


def collect(*pieces):
    arrays, where = indexed(pieces)
    whole = pl.BlockSpec(memory_space=pltpu.VMEM)
    return pl.pallas_call(
        functools.partial(collect_kernel, where, len(arrays)),
        out_shape=jax.ShapeDtypeStruct((sum(p[2] for p in where), TILE), jnp.bfloat16),
        in_specs=[whole] * len(arrays),
        out_specs=whole,
        compiler_params=limit(4),
        name="collect",
    )(*arrays)


def slots_of(v_mask):
    rows = [v_mask[a] for a in range(ABT_DEV)]
    chosen = sum(rows)
    taken = jnp.zeros_like(chosen)
    slots = [jnp.zeros_like(chosen) for _ in range(VCAP)]
    for a in range(ABT_DEV):
        slot = jnp.where(rows[a] > 0, taken, chosen + a - taken)
        taken = taken + rows[a]
        slots = [s + jnp.where(slot == j, a, 0) for j, s in enumerate(slots)]
    return jnp.stack(slots)


def product_kernel(plan, count, adds, slot_ref, own_ref, other_ref, *refs):
    arrays, refs = refs[:count], refs[count:]
    before = None
    if adds:
        before, refs = refs[0], refs[1:]
    out_ref, left, right = refs
    pair, virt = lax.axis_index("pair"), lax.axis_index("virt")
    xl, z, core = pair // NZ, pair % NZ, virt % 2
    way = 1 - 2 * core
    right[...] = jnp.zeros_like(right)
    for i, (array, base, side, across, step) in enumerate(plan):
        depth = lax.rem(z + step * way + NZ, NZ)
        k = (xl if not across else 1 - xl) * NZ + depth
        member = k // 4
        half = pl.multiple_of((k % 2) * TILE, TILE)
        mine = ((k // 2) % 2) == core
        at = pl.ds(i * TILE, TILE)
        left[:, at] = jnp.where(
            mine, own_ref[member, :, pl.ds(half, TILE)], other_ref[member, :, pl.ds(half, TILE)]
        )
        first = start(base, side, core)
        for j in range(VCAP):
            to = pl.multiple_of(slot_ref[j, k] * TILE, TILE)
            right[at, pl.ds(to, TILE)] = arrays[array][pl.ds(first + j * TILE, TILE), :]

    def columns(i, _):
        at = pl.ds(pl.multiple_of(i * 256, 256), 256)
        total = jnp.dot(left[...], right[:, at], preferred_element_type=jnp.float32)
        if before is not None:
            total = total + before[:, at]
        out_ref[:, at] = total.astype(out_ref.dtype)
        return 0

    lax.fori_loop(0, out_ref.shape[1] // 256, columns, 0)


def product(slots, t_own, t_other, chunks, before, last):
    rows, cols = t_own.shape[1], ABT_DEV * TILE
    arrays, plan = indexed(chunks)
    depth = len(plan) * TILE

    def kernel(*refs):
        product_kernel(plan, len(arrays), before is not None, *refs)

    whole = pl.BlockSpec(memory_space=pltpu.VMEM)
    args = [slots, t_own, t_other, *arrays] + ([] if before is None else [before])
    return pl.pallas_call(
        kernel,
        out_shape=jax.ShapeDtypeStruct((rows, cols), jnp.bfloat16 if last else jnp.float32),
        in_specs=[pl.BlockSpec(memory_space=pltpu.SMEM)] + [whole] * (len(args) - 1),
        out_specs=whole,
        scratch_shapes=[
            pltpu.VMEM((rows, depth), jnp.bfloat16),
            pltpu.VMEM((depth, cols), jnp.bfloat16),
        ],
        compiler_params=limit(14),
        cost_estimate=pl.CostEstimate(
            flops=2 * rows * depth * cols,
            bytes_accessed=4 * rows * cols + 2 * depth * TILE * 4,
            transcendentals=0,
        ),
    )(*args)


def both_cores(x):
    return lax.all_gather(x, "virt", axis=0, axis_index_groups=CORES, tiled=True)


def ladder(t_amps, v_ints, t_mask, v_mask):
    own, t_masked = pack(v_ints, t_amps, v_mask, t_mask, len(SAME_CORE[0]))
    side = shift(own, SIDE)
    d = {0: both_cores(own)}
    for s in range(1, 8):
        d[s] = shift(d[s - 1], RING)
    d8 = collect((d[1], 0, CHUNK, MINE))
    d8 = shift(d8, LEAP)
    t_own = lax.all_to_all(t_masked, "virt", 0, 0, axis_index_groups=SAME_CORE, tiled=True)
    t_other = shift(t_own, CORE)
    slots = slots_of(v_mask)

    x = {}
    for parts in FORWARD.values():
        arrays = [(d8, 0, CHUNK, STILL) if s == 8 else (d[s], 0, 2 * CHUNK, STILL) for s in parts]
        packed = arrays[0][0]
        if len(arrays) > 1:
            packed = collect(*arrays)
        packed = shift(packed, SIDE)
        for i, s in enumerate(parts):
            x[s] = (packed, 2 * CHUNK * i)

    def exchange(columns):
        sources = [(x[s] if across else (d[s], 0)) for s, across in columns]
        rest = collect(*((array, base, CHUNK, OTHER) for array, base in sources))
        rest = shift(rest, CORE)
        return [(rest, i * CHUNK, STILL, across, s) for i, (s, across) in enumerate(columns)]

    def direct(*columns):
        return [
            (*(x[s] if across else (d[s], 0)), MINE, across, -s) for s, across in columns
        ]

    near = exchange([(s, False) for s in range(1, 7)] + [(s, True) for s in range(1, 5)])
    end = exchange([(5, True), (6, True), (7, False), (7, True)])
    zero = [(own, 0, STILL, False, 0), (side, 0, STILL, True, 0)]
    zero += direct(*((s, False) for s in range(1, 5)), (1, True), (2, True))
    first = direct((5, False), (6, False), (3, True), (4, True)) + near
    second = direct((5, True), (6, True), (7, False), (7, True))
    second += [(d8, 0, STILL, False, -8), (*x[8], STILL, True, -8)]
    total = None
    for name, chunks in (("zero", zero), ("first", first), ("second", second), ("third", end)):
        total = product(slots, t_own, t_other, chunks, total, name == "third")
    return total


FORWARD = {"x12": (1, 2), "x38": (3, 8), "x4": (4,), "x5": (5,), "x6": (6,), "x7": (7,)}


def solution(mesh):
    return jax.shard_map(
        ladder,
        mesh=mesh,
        in_specs=(P("pair", "virt"), P("virt", "pair"), P("pair", "virt"), P("virt", None)),
        out_specs=P("pair", "virt"),
        check_vma=False,
    )
```

```python
import functools

import jax
import jax.numpy as jnp
from jax import lax
from jax.experimental import pallas as pl
from jax.experimental.pallas import tpu as pltpu
from jax.sharding import PartitionSpec as P


TILE = 128
ABT_DEV = 8
VCAP = 4
NX, NZ, NY, NH = 2, 16, 4, 2
BOTH = ("pair", "virt")
CHUNK = VCAP * TILE


def moved(to):
    pairs = []
    for xl in range(NX):
        for z in range(NZ):
            for y in range(NY):
                for xh in range(NH):
                    for c in range(2):
                        a, b, d, e, g = to(xl, z, y, xh, c)
                        source = (xl * NZ + z) * 16 + y * 4 + xh * 2 + c
                        pairs.append((source, (a * NZ + b % NZ) * 16 + d * 4 + e * 2 + g))
    return pairs


STILL, MINE, OTHER = 0, 1, 2
RING = moved(lambda xl, z, y, xh, c: (xl, z + 1 - 2 * c, y, xh, c))
LEAP = moved(lambda xl, z, y, xh, c: (xl, z + 5 - 10 * c, y, xh, c))
CORE = moved(lambda xl, z, y, xh, c: (xl, z, y, xh, 1 - c))
SIDE = moved(lambda xl, z, y, xh, c: (1 - xl, z, y, xh, c))
SAME_CORE = [[y * 4 + xh * 2 + c for y in range(NY) for xh in range(NH)] for c in range(2)]
CORES = [[y * 4 + xh * 2 + c for c in range(2)] for y in range(NY) for xh in range(NH)]


def limit(mib):
    return pltpu.CompilerParams(vmem_limit_bytes=mib * 1024 * 1024)


def shift(x, pairs):
    return lax.ppermute(x, BOTH, pairs)


def pack_kernel(v_mask_ref, t_mask_ref, v_ref, t_ref, v_out, t_out):
    column = lax.axis_index("pair")
    flags = [v_mask_ref[a, column] for a in range(ABT_DEV)]
    chosen = sum(flags)
    taken = jnp.int32(0)
    for a in range(ABT_DEV):
        slot = jnp.where(flags[a] > 0, taken, chosen + a - taken)
        taken = taken + flags[a]

        @pl.when(slot < VCAP)
        def _():
            tile = v_ref[pl.ds(a * TILE, TILE), :] * flags[a].astype(jnp.bfloat16)
            v_out[pl.ds(pl.multiple_of(slot * TILE, TILE), TILE), :] = tile.T

    for p in range(t_mask_ref.shape[1]):
        for k in range(t_mask_ref.shape[0]):
            at = (pl.ds(p * TILE, TILE), pl.ds(k * TILE, TILE))
            tile = t_ref[at] * t_mask_ref[k, p].astype(jnp.bfloat16)
            for i in range(t_out.shape[0]):
                t_out[(i, *at)] = tile


def pack(v_ints, t_amps, v_mask, t_mask, copies):
    spread = (copies, *t_amps.shape)

    def block(shape):
        return pl.BlockSpec(shape, lambda i: (0,) * len(shape))

    return pl.pallas_call(
        pack_kernel,
        grid=(1,),
        out_shape=[
            jax.ShapeDtypeStruct((CHUNK, TILE), jnp.bfloat16),
            jax.ShapeDtypeStruct(spread, jnp.bfloat16),
        ],
        in_specs=[
            pl.BlockSpec(memory_space=pltpu.SMEM),
            pl.BlockSpec(memory_space=pltpu.SMEM),
            block(v_ints.shape),
            block(t_amps.shape),
        ],
        out_specs=[block((CHUNK, TILE)), block(spread)],
        name="pack",
    )(v_mask, t_mask.T, v_ints, t_amps)


def collect_kernel(pieces, count, *refs):
    core = lax.axis_index("virt") % 2
    to = 0
    for array, base, rows, side in pieces:
        refs[count][pl.ds(to, rows), :] = refs[array][pl.ds(start(base, side, core), rows), :]
        to += rows


def start(base, side, core):
    if side == STILL:
        return base
    return pl.multiple_of(base + (core if side == MINE else 1 - core) * CHUNK, CHUNK)


def indexed(pieces):
    arrays, where = [], []
    for array, *rest in pieces:
        at = next((i for i, seen in enumerate(arrays) if seen is array), len(arrays))
        if at == len(arrays):
            arrays.append(array)
        where.append((at, *rest))
    return arrays, where


def collect(*pieces):
    arrays, where = indexed(pieces)
    whole = pl.BlockSpec(memory_space=pltpu.VMEM)
    return pl.pallas_call(
        functools.partial(collect_kernel, where, len(arrays)),
        out_shape=jax.ShapeDtypeStruct((sum(p[2] for p in where), TILE), jnp.bfloat16),
        in_specs=[whole] * len(arrays),
        out_specs=whole,
        compiler_params=limit(4),
        name="collect",
    )(*arrays)


def slots_of(v_mask):
    rows = [v_mask[a] for a in range(ABT_DEV)]
    chosen = sum(rows)
    taken = jnp.zeros_like(chosen)
    slots = [jnp.zeros_like(chosen) for _ in range(VCAP)]
    for a in range(ABT_DEV):
        slot = jnp.where(rows[a] > 0, taken, chosen + a - taken)
        taken = taken + rows[a]
        slots = [s + jnp.where(slot == j, a, 0) for j, s in enumerate(slots)]
    return jnp.stack(slots)


def product_kernel(plan, count, adds, slot_ref, own_ref, other_ref, *refs):
    arrays, refs = refs[:count], refs[count:]
    before = None
    if adds:
        before, refs = refs[0], refs[1:]
    out_ref, left, right = refs
    pair, virt = lax.axis_index("pair"), lax.axis_index("virt")
    xl, z, core = pair // NZ, pair % NZ, virt % 2
    way = 1 - 2 * core
    right[...] = jnp.zeros_like(right)
    for i, (array, base, side, across, step) in enumerate(plan):
        depth = lax.rem(z + step * way + NZ, NZ)
        k = (xl if not across else 1 - xl) * NZ + depth
        member = k // 4
        half = pl.multiple_of((k % 2) * TILE, TILE)
        mine = ((k // 2) % 2) == core
        at = pl.ds(i * TILE, TILE)
        left[:, at] = jnp.where(
            mine, own_ref[member, :, pl.ds(half, TILE)], other_ref[member, :, pl.ds(half, TILE)]
        )
        first = start(base, side, core)
        for j in range(VCAP):
            to = pl.multiple_of(slot_ref[j, k] * TILE, TILE)
            right[at, pl.ds(to, TILE)] = arrays[array][pl.ds(first + j * TILE, TILE), :]

    def columns(i, _):
        at = pl.ds(pl.multiple_of(i * 256, 256), 256)
        total = jnp.dot(left[...], right[:, at], preferred_element_type=jnp.float32)
        if before is not None:
            total = total + before[:, at]
        out_ref[:, at] = total.astype(out_ref.dtype)
        return 0

    lax.fori_loop(0, out_ref.shape[1] // 256, columns, 0)


def product(slots, t_own, t_other, chunks, before, last):
    rows, cols = t_own.shape[1], ABT_DEV * TILE
    arrays, plan = indexed(chunks)
    depth = len(plan) * TILE

    def kernel(*refs):
        product_kernel(plan, len(arrays), before is not None, *refs)

    whole = pl.BlockSpec(memory_space=pltpu.VMEM)
    args = [slots, t_own, t_other, *arrays] + ([] if before is None else [before])
    return pl.pallas_call(
        kernel,
        out_shape=jax.ShapeDtypeStruct((rows, cols), jnp.bfloat16 if last else jnp.float32),
        in_specs=[pl.BlockSpec(memory_space=pltpu.SMEM)] + [whole] * (len(args) - 1),
        out_specs=whole,
        scratch_shapes=[
            pltpu.VMEM((rows, depth), jnp.bfloat16),
            pltpu.VMEM((depth, cols), jnp.bfloat16),
        ],
        compiler_params=limit(14),
        cost_estimate=pl.CostEstimate(
            flops=2 * rows * depth * cols,
            bytes_accessed=4 * rows * cols + 2 * depth * TILE * 4,
            transcendentals=0,
        ),
    )(*args)


def both_cores(x):
    return lax.all_gather(x, "virt", axis=0, axis_index_groups=CORES, tiled=True)


def ladder(t_amps, v_ints, t_mask, v_mask):
    own, t_masked = pack(v_ints, t_amps, v_mask, t_mask, len(SAME_CORE[0]))
    side = shift(own, SIDE)
    d = {0: both_cores(own)}
    for s in range(1, 8):
        d[s] = shift(d[s - 1], RING)
    d8 = collect((d[3], 0, CHUNK, MINE))
    d8 = shift(d8, LEAP)
    t_own = lax.all_to_all(t_masked, "virt", 0, 0, axis_index_groups=SAME_CORE, tiled=True)
    t_other = shift(t_own, CORE)
    slots = slots_of(v_mask)

    x = {}
    for parts in FORWARD.values():
        arrays = [(d8, 0, CHUNK, STILL) if s == 8 else (d[s], 0, 2 * CHUNK, STILL) for s in parts]
        packed = arrays[0][0]
        if len(arrays) > 1:
            packed = collect(*arrays)
        packed = shift(packed, SIDE)
        for i, s in enumerate(parts):
            x[s] = (packed, 2 * CHUNK * i)

    def exchange(columns):
        sources = [(x[s] if across else (d[s], 0)) for s, across in columns]
        rest = collect(*((array, base, CHUNK, OTHER) for array, base in sources))
        rest = shift(rest, CORE)
        return [(rest, i * CHUNK, STILL, across, s) for i, (s, across) in enumerate(columns)]

    def direct(*columns):
        return [
            (*(x[s] if across else (d[s], 0)), MINE, across, -s) for s, across in columns
        ]

    near = exchange([(s, False) for s in range(1, 7)] + [(s, True) for s in range(1, 5)])
    end = exchange([(5, True), (6, True), (7, False), (7, True)])
    first = [(own, 0, STILL, False, 0), (side, 0, STILL, True, 0)] + near
    first += direct(*((s, False) for s in range(1, 7)), *((s, True) for s in range(1, 5)))
    second = direct((5, True), (6, True), (7, False), (7, True))
    second += [(d8, 0, STILL, False, -8), (*x[8], STILL, True, -8)]
    total = None
    for name, chunks in (("first", first), ("second", second), ("third", end)):
        total = product(slots, t_own, t_other, chunks, total, name == "third")
    return total


FORWARD = {"x12": (1, 2), "x34": (3, 4), "x58": (5, 8), "x6": (6,), "x7": (7,)}


def solution(mesh):
    return jax.shard_map(
        ladder,
        mesh=mesh,
        in_specs=(P("pair", "virt"), P("virt", "pair"), P("pair", "virt"), P("virt", None)),
        out_specs=P("pair", "virt"),
        check_vma=False,
    )
```

```python
import functools

import jax
import jax.numpy as jnp
from jax import lax
from jax.experimental import pallas as pl
from jax.experimental.pallas import tpu as pltpu
from jax.sharding import PartitionSpec as P


TILE = 128
ABT_DEV = 8
VCAP = 4
NX, NZ, NY, NH = 2, 16, 4, 2
BOTH = ("pair", "virt")
CHUNK = VCAP * TILE


def moved(to):
    pairs = []
    for xl in range(NX):
        for z in range(NZ):
            for y in range(NY):
                for xh in range(NH):
                    for c in range(2):
                        a, b, d, e, g = to(xl, z, y, xh, c)
                        source = (xl * NZ + z) * 16 + y * 4 + xh * 2 + c
                        pairs.append((source, (a * NZ + b % NZ) * 16 + d * 4 + e * 2 + g))
    return pairs


STILL, MINE, OTHER = 0, 1, 2
RING = moved(lambda xl, z, y, xh, c: (xl, z + 1 - 2 * c, y, xh, c))
LEAP = moved(lambda xl, z, y, xh, c: (xl, z + 5 - 10 * c, y, xh, c))
CORE = moved(lambda xl, z, y, xh, c: (xl, z, y, xh, 1 - c))
SIDE = moved(lambda xl, z, y, xh, c: (1 - xl, z, y, xh, c))
SAME_CORE = [[y * 4 + xh * 2 + c for y in range(NY) for xh in range(NH)] for c in range(2)]
CORES = [[y * 4 + xh * 2 + c for c in range(2)] for y in range(NY) for xh in range(NH)]


def limit(mib):
    return pltpu.CompilerParams(vmem_limit_bytes=mib * 1024 * 1024)


def shift(x, pairs):
    return lax.ppermute(x, BOTH, pairs)


def pack_kernel(v_mask_ref, t_mask_ref, rows_ref, v_ref, t_ref, v_out, t_out, table_out):
    before = jnp.zeros_like(rows_ref[pl.ds(0, 1), :])
    for a in range(ABT_DEV):
        row = rows_ref[pl.ds(a, 1), :]
        table_out[pl.ds(a, 1), :] = before * row
        table_out[pl.ds(ABT_DEV + a, 1), :] = row
        before = before + row
    column = lax.axis_index("pair")
    flags = [v_mask_ref[a, column] for a in range(ABT_DEV)]
    chosen = sum(flags)
    taken = jnp.int32(0)
    for a in range(ABT_DEV):
        slot = jnp.where(flags[a] > 0, taken, chosen + a - taken)
        taken = taken + flags[a]

        @pl.when(slot < VCAP)
        def _():
            tile = v_ref[pl.ds(a * TILE, TILE), :] * flags[a].astype(jnp.bfloat16)
            v_out[pl.ds(pl.multiple_of(slot * TILE, TILE), TILE), :] = tile.T

    for p in range(t_mask_ref.shape[1]):
        for k in range(t_mask_ref.shape[0]):
            at = (pl.ds(p * TILE, TILE), pl.ds(k * TILE, TILE))
            tile = t_ref[at] * t_mask_ref[k, p].astype(jnp.bfloat16)
            for i in range(t_out.shape[0]):
                t_out[(i, *at)] = tile


def pack(v_ints, t_amps, v_mask, t_mask, copies):
    spread = (copies, *t_amps.shape)

    def block(shape):
        return pl.BlockSpec(shape, lambda i: (0,) * len(shape))

    return pl.pallas_call(
        pack_kernel,
        grid=(1,),
        out_shape=[
            jax.ShapeDtypeStruct((CHUNK, TILE), jnp.bfloat16),
            jax.ShapeDtypeStruct(spread, jnp.bfloat16),
            jax.ShapeDtypeStruct((2 * v_mask.shape[0], v_mask.shape[1]), jnp.int32),
        ],
        in_specs=[
            pl.BlockSpec(memory_space=pltpu.SMEM),
            pl.BlockSpec(memory_space=pltpu.SMEM),
            block(v_mask.shape),
            block(v_ints.shape),
            block(t_amps.shape),
        ],
        out_specs=[
            block((CHUNK, TILE)),
            block(spread),
            block((2 * v_mask.shape[0], v_mask.shape[1])),
        ],
        name="pack",
    )(v_mask, t_mask.T, v_mask, v_ints, t_amps)


def collect_kernel(pieces, count, *refs):
    core = lax.axis_index("virt") % 2
    to = 0
    for array, base, rows, side in pieces:
        refs[count][pl.ds(to, rows), :] = refs[array][pl.ds(start(base, side, core), rows), :]
        to += rows


def start(base, side, core):
    if side == STILL:
        return base
    return pl.multiple_of(base + (core if side == MINE else 1 - core) * CHUNK, CHUNK)


def indexed(pieces):
    arrays, where = [], []
    for array, *rest in pieces:
        at = next((i for i, seen in enumerate(arrays) if seen is array), len(arrays))
        if at == len(arrays):
            arrays.append(array)
        where.append((at, *rest))
    return arrays, where


def collect(*pieces):
    arrays, where = indexed(pieces)
    whole = pl.BlockSpec(memory_space=pltpu.VMEM)
    return pl.pallas_call(
        functools.partial(collect_kernel, where, len(arrays)),
        out_shape=jax.ShapeDtypeStruct((sum(p[2] for p in where), TILE), jnp.bfloat16),
        in_specs=[whole] * len(arrays),
        out_specs=whole,
        compiler_params=limit(4),
        name="collect",
    )(*arrays)


def product_kernel(plan, count, adds, last, table_ref, own_ref, other_ref, *refs):
    arrays, refs = refs[:count], refs[count:]
    before = None
    if adds:
        before, refs = refs[0], refs[1:]
    out_ref, left, right, table, sem = refs[:5]
    load = pltpu.make_async_copy(table_ref, table, sem)
    load.start()
    pair, virt = lax.axis_index("pair"), lax.axis_index("virt")
    xl, z, core = pair // NZ, pair % NZ, virt % 2
    way = 1 - 2 * core

    def column(across, step):
        return (xl if not across else 1 - xl) * NZ + lax.rem(z + step * way + NZ, NZ)

    for i, (_, _, _, across, step) in enumerate(plan):
        k = column(across, step)
        member = k // 4
        half = pl.multiple_of((k % 2) * TILE, TILE)
        mine = ((k // 2) % 2) == core
        left[:, pl.ds(i * TILE, TILE)] = jnp.where(
            mine, own_ref[member, :, pl.ds(half, TILE)], other_ref[member, :, pl.ds(half, TILE)]
        )
    load.wait()
    for i, (array, base, side, across, step) in enumerate(plan):
        k = column(across, step)
        first = start(base, side, core)
        for a in range(ABT_DEV):
            tile = arrays[array][pl.ds(pl.multiple_of(first + table[a, k] * TILE, TILE), TILE), :]
            flag = table[ABT_DEV + a, k].astype(jnp.bfloat16)
            right[pl.ds(i * TILE, TILE), pl.ds(a * TILE, TILE)] = tile * flag
    sends = []
    for i in range(ABT_DEV * TILE // 256):
        at = pl.ds(i * 256, 256)
        total = jnp.dot(left[...], right[:, at], preferred_element_type=jnp.float32)
        if before is not None:
            total = total + before[:, at]
        if not last:
            out_ref[:, at] = total
            continue
        stage, sems = refs[5:]
        stage[:, at] = total.astype(stage.dtype)
        sends.append(pltpu.make_async_copy(stage.at[:, at], out_ref.at[:, at], sems.at[i]))
        sends[-1].start()
    for send in sends:
        send.wait()


def product(table, t_own, t_other, chunks, before, last):
    rows, cols = t_own.shape[1], ABT_DEV * TILE
    arrays, plan = indexed(chunks)
    depth = len(plan) * TILE

    def kernel(*refs):
        product_kernel(plan, len(arrays), before is not None, last, *refs)

    whole, anywhere = pl.BlockSpec(memory_space=pltpu.VMEM), pl.BlockSpec(memory_space=pl.ANY)
    args = [table, t_own, t_other, *arrays] + ([] if before is None else [before])
    scratch = [
        pltpu.VMEM((rows, depth), jnp.bfloat16),
        pltpu.VMEM((depth, cols), jnp.bfloat16),
        pltpu.SMEM(table.shape, jnp.int32),
        pltpu.SemaphoreType.DMA,
    ]
    if last:
        scratch += [pltpu.VMEM((rows, cols), jnp.bfloat16), pltpu.SemaphoreType.DMA((cols // 256,))]
    return pl.pallas_call(
        kernel,
        out_shape=jax.ShapeDtypeStruct((rows, cols), jnp.bfloat16 if last else jnp.float32),
        in_specs=[anywhere] + [whole] * (len(args) - 1),
        out_specs=anywhere if last else whole,
        scratch_shapes=scratch,
        compiler_params=limit(14),
        cost_estimate=pl.CostEstimate(
            flops=2 * rows * depth * cols,
            bytes_accessed=4 * rows * cols + 2 * depth * TILE * 4,
            transcendentals=0,
        ),
    )(*args)


def both_cores(x):
    return lax.all_gather(x, "virt", axis=0, axis_index_groups=CORES, tiled=True)


def ladder(t_amps, v_ints, t_mask, v_mask):
    own, t_masked, table = pack(v_ints, t_amps, v_mask, t_mask, len(SAME_CORE[0]))
    side = shift(own, SIDE)
    d = {0: both_cores(own)}
    for s in range(1, 8):
        d[s] = shift(d[s - 1], RING)
    d8 = collect((d[3], 0, CHUNK, MINE))
    d8 = shift(d8, LEAP)
    t_own = lax.all_to_all(t_masked, "virt", 0, 0, axis_index_groups=SAME_CORE, tiled=True)
    t_other = shift(t_own, CORE)

    x = {}
    for parts in FORWARD.values():
        arrays = [(d8, 0, CHUNK, STILL) if s == 8 else (d[s], 0, 2 * CHUNK, STILL) for s in parts]
        packed = arrays[0][0]
        if len(arrays) > 1:
            packed = collect(*arrays)
        packed = shift(packed, SIDE)
        for i, s in enumerate(parts):
            x[s] = (packed, 2 * CHUNK * i)

    def exchange(columns):
        sources = [(x[s] if across else (d[s], 0)) for s, across in columns]
        rest = collect(*((array, base, CHUNK, OTHER) for array, base in sources))
        rest = shift(rest, CORE)
        return [(rest, i * CHUNK, STILL, across, s) for i, (s, across) in enumerate(columns)]

    def direct(*columns):
        return [
            (*(x[s] if across else (d[s], 0)), MINE, across, -s) for s, across in columns
        ]

    near = exchange([(s, False) for s in range(1, 7)] + [(s, True) for s in range(1, 5)])
    end = exchange([(5, True), (6, True), (7, False), (7, True)])
    first = [(own, 0, STILL, False, 0), (side, 0, STILL, True, 0)] + near
    first += direct(*((s, False) for s in range(1, 7)), *((s, True) for s in range(1, 5)))
    second = direct((5, True), (6, True), (7, False), (7, True))
    second += [(d8, 0, STILL, False, -8), (*x[8], STILL, True, -8)]
    total = None
    for name, chunks in (("first", first), ("second", second), ("third", end)):
        total = product(table, t_own, t_other, chunks, total, name == "third")
    return total


FORWARD = {"x12": (1, 2), "x34": (3, 4), "x58": (5, 8), "x6": (6,), "x7": (7,)}


def solution(mesh):
    return jax.shard_map(
        ladder,
        mesh=mesh,
        in_specs=(P("pair", "virt"), P("virt", "pair"), P("pair", "virt"), P("virt", None)),
        out_specs=P("pair", "virt"),
        check_vma=False,
    )
```

```python
import functools

import jax
import jax.numpy as jnp
from jax import lax
from jax.experimental import pallas as pl
from jax.experimental.pallas import tpu as pltpu
from jax.sharding import PartitionSpec as P


TILE = 128
ABT_DEV = 8
VCAP = 4
NX, NZ, NY, NH = 2, 16, 4, 2
BOTH = ("pair", "virt")
CHUNK = VCAP * TILE


def moved(to):
    pairs = []
    for xl in range(NX):
        for z in range(NZ):
            for y in range(NY):
                for xh in range(NH):
                    for c in range(2):
                        a, b, d, e, g = to(xl, z, y, xh, c)
                        source = (xl * NZ + z) * 16 + y * 4 + xh * 2 + c
                        pairs.append((source, (a * NZ + b % NZ) * 16 + d * 4 + e * 2 + g))
    return pairs


STILL, MINE, OTHER = 0, 1, 2
RING = moved(lambda xl, z, y, xh, c: (xl, z + 1 - 2 * c, y, xh, c))
LEAP = moved(lambda xl, z, y, xh, c: (xl, z + 5 - 10 * c, y, xh, c))
CORE = moved(lambda xl, z, y, xh, c: (xl, z, y, xh, 1 - c))
SIDE = moved(lambda xl, z, y, xh, c: (1 - xl, z, y, xh, c))
SAME_CORE = [[y * 4 + xh * 2 + c for y in range(NY) for xh in range(NH)] for c in range(2)]
CORES = [[y * 4 + xh * 2 + c for c in range(2)] for y in range(NY) for xh in range(NH)]


def limit(mib):
    return pltpu.CompilerParams(vmem_limit_bytes=mib * 1024 * 1024)


def shift(x, pairs):
    return lax.ppermute(x, BOTH, pairs)


def pack_kernel(
    v_mask_ref, t_mask_ref, rows_ref, v_ref, t_ref, v_out, t_out, table_out, masked, sems
):
    for p in range(t_mask_ref.shape[1]):
        for k in range(t_mask_ref.shape[0]):
            at = (pl.ds(p * TILE, TILE), pl.ds(k * TILE, TILE))
            masked[at] = t_ref[at] * t_mask_ref[k, p].astype(jnp.bfloat16)
    sends = [pltpu.make_async_copy(masked, t_out.at[i], sems.at[i]) for i in range(t_out.shape[0])]
    before = jnp.zeros_like(rows_ref[pl.ds(0, 1), :])
    for a in range(ABT_DEV):
        row = rows_ref[pl.ds(a, 1), :]
        table_out[pl.ds(a, 1), :] = before * row
        table_out[pl.ds(ABT_DEV + a, 1), :] = row
        before = before + row
    for send in sends:
        send.start()
    column = lax.axis_index("pair")
    flags = [v_mask_ref[a, column] for a in range(ABT_DEV)]
    chosen = sum(flags)
    taken = jnp.int32(0)
    for a in range(ABT_DEV):
        slot = jnp.where(flags[a] > 0, taken, chosen + a - taken)
        taken = taken + flags[a]

        @pl.when(slot < VCAP)
        def _():
            tile = v_ref[pl.ds(a * TILE, TILE), :] * flags[a].astype(jnp.bfloat16)
            v_out[pl.ds(pl.multiple_of(slot * TILE, TILE), TILE), :] = tile.T

    for send in sends:
        send.wait()


def pack(v_ints, t_amps, v_mask, t_mask, copies):
    spread = (copies, *t_amps.shape)

    def block(shape):
        return pl.BlockSpec(shape, lambda i: (0,) * len(shape))

    return pl.pallas_call(
        pack_kernel,
        grid=(1,),
        out_shape=[
            jax.ShapeDtypeStruct((CHUNK, TILE), jnp.bfloat16),
            jax.ShapeDtypeStruct(spread, jnp.bfloat16),
            jax.ShapeDtypeStruct((2 * v_mask.shape[0], v_mask.shape[1]), jnp.int32),
        ],
        in_specs=[
            pl.BlockSpec(memory_space=pltpu.SMEM),
            pl.BlockSpec(memory_space=pltpu.SMEM),
            block(v_mask.shape),
            block(v_ints.shape),
            block(t_amps.shape),
        ],
        out_specs=[
            block((CHUNK, TILE)),
            pl.BlockSpec(memory_space=pl.ANY),
            block((2 * v_mask.shape[0], v_mask.shape[1])),
        ],
        scratch_shapes=[
            pltpu.VMEM(t_amps.shape, jnp.bfloat16),
            pltpu.SemaphoreType.DMA((copies,)),
        ],
        name="pack",
    )(v_mask, t_mask.T, v_mask, v_ints, t_amps)


def collect_kernel(pieces, count, *refs):
    core = lax.axis_index("virt") % 2
    to = 0
    for array, base, rows, side in pieces:
        refs[count][pl.ds(to, rows), :] = refs[array][pl.ds(start(base, side, core), rows), :]
        to += rows


def start(base, side, core):
    if side == STILL:
        return base
    return pl.multiple_of(base + (core if side == MINE else 1 - core) * CHUNK, CHUNK)


def indexed(pieces):
    arrays, where = [], []
    for array, *rest in pieces:
        at = next((i for i, seen in enumerate(arrays) if seen is array), len(arrays))
        if at == len(arrays):
            arrays.append(array)
        where.append((at, *rest))
    return arrays, where


def collect(*pieces):
    arrays, where = indexed(pieces)
    whole = pl.BlockSpec(memory_space=pltpu.VMEM)
    return pl.pallas_call(
        functools.partial(collect_kernel, where, len(arrays)),
        out_shape=jax.ShapeDtypeStruct((sum(p[2] for p in where), TILE), jnp.bfloat16),
        in_specs=[whole] * len(arrays),
        out_specs=whole,
        compiler_params=limit(4),
        name="collect",
    )(*arrays)


def product_kernel(plan, count, adds, last, table_ref, own_ref, other_ref, *refs):
    arrays, refs = refs[:count], refs[count:]
    before = None
    if adds:
        before, refs = refs[0], refs[1:]
    out_ref, left, right, table, sem = refs[:5]
    load = pltpu.make_async_copy(table_ref, table, sem)
    load.start()
    pair, virt = lax.axis_index("pair"), lax.axis_index("virt")
    xl, z, core = pair // NZ, pair % NZ, virt % 2
    way = 1 - 2 * core

    def column(across, step):
        return (xl if not across else 1 - xl) * NZ + lax.rem(z + step * way + NZ, NZ)

    for i, (_, _, _, across, step) in enumerate(plan):
        k = column(across, step)
        member = k // 4
        half = pl.multiple_of((k % 2) * TILE, TILE)
        mine = ((k // 2) % 2) == core
        left[:, pl.ds(i * TILE, TILE)] = jnp.where(
            mine, own_ref[member, :, pl.ds(half, TILE)], other_ref[member, :, pl.ds(half, TILE)]
        )
    load.wait()
    for i, (array, base, side, across, step) in enumerate(plan):
        k = column(across, step)
        first = start(base, side, core)
        for a in range(ABT_DEV):
            tile = arrays[array][pl.ds(pl.multiple_of(first + table[a, k] * TILE, TILE), TILE), :]
            flag = table[ABT_DEV + a, k].astype(jnp.bfloat16)
            right[pl.ds(i * TILE, TILE), pl.ds(a * TILE, TILE)] = tile * flag
    sends = []
    for i in range(ABT_DEV * TILE // 256):
        at = pl.ds(i * 256, 256)
        total = jnp.dot(left[...], right[:, at], preferred_element_type=jnp.float32)
        if before is not None:
            total = total + before[:, at]
        if not last:
            out_ref[:, at] = total
            continue
        stage, sems = refs[5:]
        stage[:, at] = total.astype(stage.dtype)
        sends.append(pltpu.make_async_copy(stage.at[:, at], out_ref.at[:, at], sems.at[i]))
        sends[-1].start()
    for send in sends:
        send.wait()


def product(table, t_own, t_other, chunks, before, last):
    rows, cols = t_own.shape[1], ABT_DEV * TILE
    arrays, plan = indexed(chunks)
    depth = len(plan) * TILE

    def kernel(*refs):
        product_kernel(plan, len(arrays), before is not None, last, *refs)

    whole, anywhere = pl.BlockSpec(memory_space=pltpu.VMEM), pl.BlockSpec(memory_space=pl.ANY)
    args = [table, t_own, t_other, *arrays] + ([] if before is None else [before])
    scratch = [
        pltpu.VMEM((rows, depth), jnp.bfloat16),
        pltpu.VMEM((depth, cols), jnp.bfloat16),
        pltpu.SMEM(table.shape, jnp.int32),
        pltpu.SemaphoreType.DMA,
    ]
    if last:
        scratch += [pltpu.VMEM((rows, cols), jnp.bfloat16), pltpu.SemaphoreType.DMA((cols // 256,))]
    return pl.pallas_call(
        kernel,
        out_shape=jax.ShapeDtypeStruct((rows, cols), jnp.bfloat16 if last else jnp.float32),
        in_specs=[anywhere] + [whole] * (len(args) - 1),
        out_specs=anywhere if last else whole,
        scratch_shapes=scratch,
        compiler_params=limit(14),
        cost_estimate=pl.CostEstimate(
            flops=2 * rows * depth * cols,
            bytes_accessed=4 * rows * cols + 2 * depth * TILE * 4,
            transcendentals=0,
        ),
    )(*args)


def both_cores(x):
    return lax.all_gather(x, "virt", axis=0, axis_index_groups=CORES, tiled=True)


def ladder(t_amps, v_ints, t_mask, v_mask):
    own, t_masked, table = pack(v_ints, t_amps, v_mask, t_mask, len(SAME_CORE[0]))
    side = shift(own, SIDE)
    d = {0: both_cores(own)}
    for s in range(1, 8):
        d[s] = shift(d[s - 1], RING)
    d8 = collect((d[3], 0, CHUNK, MINE))
    d8 = shift(d8, LEAP)
    t_own = lax.all_to_all(t_masked, "virt", 0, 0, axis_index_groups=SAME_CORE, tiled=True)
    t_other = shift(t_own, CORE)

    x = {}
    for parts in FORWARD.values():
        arrays = [(d8, 0, CHUNK, STILL) if s == 8 else (d[s], 0, 2 * CHUNK, STILL) for s in parts]
        packed = arrays[0][0]
        if len(arrays) > 1:
            packed = collect(*arrays)
        packed = shift(packed, SIDE)
        for i, s in enumerate(parts):
            x[s] = (packed, 2 * CHUNK * i)

    def exchange(columns):
        sources = [(x[s] if across else (d[s], 0)) for s, across in columns]
        rest = collect(*((array, base, CHUNK, OTHER) for array, base in sources))
        rest = shift(rest, CORE)
        return [(rest, i * CHUNK, STILL, across, s) for i, (s, across) in enumerate(columns)]

    def direct(*columns):
        return [
            (*(x[s] if across else (d[s], 0)), MINE, across, -s) for s, across in columns
        ]

    near = exchange([(s, False) for s in range(1, 7)] + [(s, True) for s in range(1, 5)])
    end = exchange([(5, True), (6, True), (7, False), (7, True)])
    first = [(own, 0, STILL, False, 0), (side, 0, STILL, True, 0)] + near
    first += direct(*((s, False) for s in range(1, 7)), *((s, True) for s in range(1, 5)))
    second = direct((5, True), (6, True), (7, False), (7, True))
    second += [(d8, 0, STILL, False, -8), (*x[8], STILL, True, -8)]
    total = None
    for name, chunks in (("first", first), ("second", second), ("third", end)):
        total = product(table, t_own, t_other, chunks, total, name == "third")
    return total


FORWARD = {"x12": (1, 2), "x34": (3, 4), "x58": (5, 8), "x6": (6,), "x7": (7,)}


def solution(mesh):
    return jax.shard_map(
        ladder,
        mesh=mesh,
        in_specs=(P("pair", "virt"), P("virt", "pair"), P("pair", "virt"), P("virt", None)),
        out_specs=P("pair", "virt"),
        check_vma=False,
    )
```

```python
import functools

import jax
import jax.numpy as jnp
from jax import lax
from jax.experimental import pallas as pl
from jax.experimental.pallas import tpu as pltpu
from jax.sharding import PartitionSpec as P


TILE = 128
ABT_DEV = 8
VCAP = 4
NX, NZ, NY, NH = 2, 16, 4, 2
BOTH = ("pair", "virt")
CHUNK = VCAP * TILE


def moved(to):
    pairs = []
    for xl in range(NX):
        for z in range(NZ):
            for y in range(NY):
                for xh in range(NH):
                    for c in range(2):
                        a, b, d, e, g = to(xl, z, y, xh, c)
                        source = (xl * NZ + z) * 16 + y * 4 + xh * 2 + c
                        pairs.append((source, (a * NZ + b % NZ) * 16 + d * 4 + e * 2 + g))
    return pairs


STILL, MINE, OTHER = 0, 1, 2
RING = moved(lambda xl, z, y, xh, c: (xl, z + 1 - 2 * c, y, xh, c))
LEAP = moved(lambda xl, z, y, xh, c: (xl, z + 4 - 8 * c, y, xh, c))
CORE = moved(lambda xl, z, y, xh, c: (xl, z, y, xh, 1 - c))
SIDE = moved(lambda xl, z, y, xh, c: (1 - xl, z, y, xh, c))
SAME_CORE = [[y * 4 + xh * 2 + c for y in range(NY) for xh in range(NH)] for c in range(2)]
CORES = [[y * 4 + xh * 2 + c for c in range(2)] for y in range(NY) for xh in range(NH)]


def limit(mib):
    return pltpu.CompilerParams(vmem_limit_bytes=mib * 1024 * 1024)


def shift(x, pairs):
    return lax.ppermute(x, BOTH, pairs)


def pack_kernel(
    v_mask_ref, t_mask_ref, rows_ref, v_ref, t_ref, v_out, t_out, table_out, masked, sems
):
    for p in range(t_mask_ref.shape[1]):
        for k in range(t_mask_ref.shape[0]):
            at = (pl.ds(p * TILE, TILE), pl.ds(k * TILE, TILE))
            masked[at] = t_ref[at] * t_mask_ref[k, p].astype(jnp.bfloat16)
    sends = [pltpu.make_async_copy(masked, t_out.at[i], sems.at[i]) for i in range(t_out.shape[0])]
    before = jnp.zeros_like(rows_ref[pl.ds(0, 1), :])
    for a in range(ABT_DEV):
        row = rows_ref[pl.ds(a, 1), :]
        table_out[pl.ds(a, 1), :] = before * row
        table_out[pl.ds(ABT_DEV + a, 1), :] = row
        before = before + row
    for send in sends:
        send.start()
    column = lax.axis_index("pair")
    flags = [v_mask_ref[a, column] for a in range(ABT_DEV)]
    chosen = sum(flags)
    taken = jnp.int32(0)
    for a in range(ABT_DEV):
        slot = jnp.where(flags[a] > 0, taken, chosen + a - taken)
        taken = taken + flags[a]

        @pl.when(slot < VCAP)
        def _():
            tile = v_ref[pl.ds(a * TILE, TILE), :] * flags[a].astype(jnp.bfloat16)
            v_out[pl.ds(pl.multiple_of(slot * TILE, TILE), TILE), :] = tile.T

    for send in sends:
        send.wait()


def pack(v_ints, t_amps, v_mask, t_mask, copies):
    spread = (copies, *t_amps.shape)

    def block(shape):
        return pl.BlockSpec(shape, lambda i: (0,) * len(shape))

    return pl.pallas_call(
        pack_kernel,
        grid=(1,),
        out_shape=[
            jax.ShapeDtypeStruct((CHUNK, TILE), jnp.bfloat16),
            jax.ShapeDtypeStruct(spread, jnp.bfloat16),
            jax.ShapeDtypeStruct((2 * v_mask.shape[0], v_mask.shape[1]), jnp.int32),
        ],
        in_specs=[
            pl.BlockSpec(memory_space=pltpu.SMEM),
            pl.BlockSpec(memory_space=pltpu.SMEM),
            block(v_mask.shape),
            block(v_ints.shape),
            block(t_amps.shape),
        ],
        out_specs=[
            block((CHUNK, TILE)),
            pl.BlockSpec(memory_space=pl.ANY),
            block((2 * v_mask.shape[0], v_mask.shape[1])),
        ],
        scratch_shapes=[
            pltpu.VMEM(t_amps.shape, jnp.bfloat16),
            pltpu.SemaphoreType.DMA((copies,)),
        ],
        name="pack",
    )(v_mask, t_mask.T, v_mask, v_ints, t_amps)


def collect_kernel(pieces, count, *refs):
    core = lax.axis_index("virt") % 2
    to = 0
    for array, base, rows, side in pieces:
        refs[count][pl.ds(to, rows), :] = refs[array][pl.ds(start(base, side, core), rows), :]
        to += rows


def start(base, side, core):
    if side == STILL:
        return base
    return pl.multiple_of(base + (core if side == MINE else 1 - core) * CHUNK, CHUNK)


def indexed(pieces):
    arrays, where = [], []
    for array, *rest in pieces:
        at = next((i for i, seen in enumerate(arrays) if seen is array), len(arrays))
        if at == len(arrays):
            arrays.append(array)
        where.append((at, *rest))
    return arrays, where


def collect(*pieces):
    arrays, where = indexed(pieces)
    whole = pl.BlockSpec(memory_space=pltpu.VMEM)
    return pl.pallas_call(
        functools.partial(collect_kernel, where, len(arrays)),
        out_shape=jax.ShapeDtypeStruct((sum(p[2] for p in where), TILE), jnp.bfloat16),
        in_specs=[whole] * len(arrays),
        out_specs=whole,
        compiler_params=limit(4),
        name="collect",
    )(*arrays)


def product_kernel(plan, count, adds, last, table_ref, own_ref, other_ref, *refs):
    arrays, refs = refs[:count], refs[count:]
    before = None
    if adds:
        before, refs = refs[0], refs[1:]
    out_ref, left, right, table, sem = refs[:5]
    load = pltpu.make_async_copy(table_ref, table, sem)
    load.start()
    pair, virt = lax.axis_index("pair"), lax.axis_index("virt")
    xl, z, core = pair // NZ, pair % NZ, virt % 2
    way = 1 - 2 * core

    def column(across, step):
        return (xl if not across else 1 - xl) * NZ + lax.rem(z + step * way + NZ, NZ)

    for i, (_, _, _, across, step) in enumerate(plan):
        k = column(across, step)
        member = k // 4
        half = pl.multiple_of((k % 2) * TILE, TILE)
        mine = ((k // 2) % 2) == core
        left[:, pl.ds(i * TILE, TILE)] = jnp.where(
            mine, own_ref[member, :, pl.ds(half, TILE)], other_ref[member, :, pl.ds(half, TILE)]
        )
    load.wait()
    for i, (array, base, side, across, step) in enumerate(plan):
        k = column(across, step)
        first = start(base, side, core)
        for a in range(ABT_DEV):
            tile = arrays[array][pl.ds(pl.multiple_of(first + table[a, k] * TILE, TILE), TILE), :]
            flag = table[ABT_DEV + a, k].astype(jnp.bfloat16)
            right[pl.ds(i * TILE, TILE), pl.ds(a * TILE, TILE)] = tile * flag
    sends = []
    for i in range(ABT_DEV * TILE // 256):
        at = pl.ds(i * 256, 256)
        total = jnp.dot(left[...], right[:, at], preferred_element_type=jnp.float32)
        if before is not None:
            total = total + before[:, at]
        if not last:
            out_ref[:, at] = total
            continue
        stage, sems = refs[5:]
        stage[:, at] = total.astype(stage.dtype)
        sends.append(pltpu.make_async_copy(stage.at[:, at], out_ref.at[:, at], sems.at[i]))
        sends[-1].start()
    for send in sends:
        send.wait()


def product(table, t_own, t_other, chunks, before, last):
    rows, cols = t_own.shape[1], ABT_DEV * TILE
    arrays, plan = indexed(chunks)
    depth = len(plan) * TILE

    def kernel(*refs):
        product_kernel(plan, len(arrays), before is not None, last, *refs)

    whole, anywhere = pl.BlockSpec(memory_space=pltpu.VMEM), pl.BlockSpec(memory_space=pl.ANY)
    args = [table, t_own, t_other, *arrays] + ([] if before is None else [before])
    scratch = [
        pltpu.VMEM((rows, depth), jnp.bfloat16),
        pltpu.VMEM((depth, cols), jnp.bfloat16),
        pltpu.SMEM(table.shape, jnp.int32),
        pltpu.SemaphoreType.DMA,
    ]
    if last:
        scratch += [pltpu.VMEM((rows, cols), jnp.bfloat16), pltpu.SemaphoreType.DMA((cols // 256,))]
    return pl.pallas_call(
        kernel,
        out_shape=jax.ShapeDtypeStruct((rows, cols), jnp.bfloat16 if last else jnp.float32),
        in_specs=[anywhere] + [whole] * (len(args) - 1),
        out_specs=anywhere if last else whole,
        scratch_shapes=scratch,
        compiler_params=limit(14),
        cost_estimate=pl.CostEstimate(
            flops=2 * rows * depth * cols,
            bytes_accessed=4 * rows * cols + 2 * depth * TILE * 4,
            transcendentals=0,
        ),
    )(*args)


def both_cores(x):
    return lax.all_gather(x, "virt", axis=0, axis_index_groups=CORES, tiled=True)


def ladder(t_amps, v_ints, t_mask, v_mask):
    own, t_masked, table = pack(v_ints, t_amps, v_mask, t_mask, len(SAME_CORE[0]))
    side = shift(own, SIDE)
    d = {0: both_cores(own)}
    for s in range(1, 8):
        d[s] = shift(d[s - 1], RING)
    d8 = collect((d[4], 0, CHUNK, MINE))
    d8 = shift(d8, LEAP)
    t_own = lax.all_to_all(t_masked, "virt", 0, 0, axis_index_groups=SAME_CORE, tiled=True)
    t_other = shift(t_own, CORE)

    x = {}
    for parts in FORWARD.values():
        arrays = [(d8, 0, CHUNK, STILL) if s == 8 else (d[s], 0, 2 * CHUNK, STILL) for s in parts]
        packed = arrays[0][0]
        if len(arrays) > 1:
            packed = collect(*arrays)
        packed = shift(packed, SIDE)
        for i, s in enumerate(parts):
            x[s] = (packed, 2 * CHUNK * i)

    def exchange(columns):
        sources = [(x[s] if across else (d[s], 0)) for s, across in columns]
        rest = collect(*((array, base, CHUNK, OTHER) for array, base in sources))
        rest = shift(rest, CORE)
        return [(rest, i * CHUNK, STILL, across, s) for i, (s, across) in enumerate(columns)]

    def direct(*columns):
        return [
            (*(x[s] if across else (d[s], 0)), MINE, across, -s) for s, across in columns
        ]

    near = exchange([(s, False) for s in range(1, 7)] + [(s, True) for s in range(1, 5)])
    end = exchange([(5, True), (6, True), (7, False), (7, True)])
    first = [(own, 0, STILL, False, 0), (side, 0, STILL, True, 0)] + near
    first += direct(*((s, False) for s in range(1, 7)), *((s, True) for s in range(1, 5)))
    second = direct((5, True), (6, True), (7, False), (7, True))
    second += [(d8, 0, STILL, False, -8), (*x[8], STILL, True, -8)]
    total = None
    for name, chunks in (("first", first), ("second", second), ("third", end)):
        total = product(table, t_own, t_other, chunks, total, name == "third")
    return total


FORWARD = {"x12": (1, 2), "x3": (3,), "x4": (4,), "x58": (5, 8), "x6": (6,), "x7": (7,)}


def solution(mesh):
    return jax.shard_map(
        ladder,
        mesh=mesh,
        in_specs=(P("pair", "virt"), P("virt", "pair"), P("pair", "virt"), P("virt", None)),
        out_specs=P("pair", "virt"),
        check_vma=False,
    )
```

```python
import functools

import jax
import jax.numpy as jnp
from jax import lax
from jax.experimental import pallas as pl
from jax.experimental.pallas import tpu as pltpu
from jax.sharding import PartitionSpec as P


TILE = 128
ABT_DEV = 8
VCAP = 4
NX, NZ, NY, NH = 2, 16, 4, 2
BOTH = ("pair", "virt")
CHUNK = VCAP * TILE


def moved(to):
    pairs = []
    for xl in range(NX):
        for z in range(NZ):
            for y in range(NY):
                for xh in range(NH):
                    for c in range(2):
                        a, b, d, e, g = to(xl, z, y, xh, c)
                        source = (xl * NZ + z) * 16 + y * 4 + xh * 2 + c
                        pairs.append((source, (a * NZ + b % NZ) * 16 + d * 4 + e * 2 + g))
    return pairs


STILL, MINE, OTHER = 0, 1, 2
RING = moved(lambda xl, z, y, xh, c: (xl, z + 1 - 2 * c, y, xh, c))
LEAP = moved(lambda xl, z, y, xh, c: (xl, z + 5 - 10 * c, y, xh, c))
CORE = moved(lambda xl, z, y, xh, c: (xl, z, y, xh, 1 - c))
SIDE = moved(lambda xl, z, y, xh, c: (1 - xl, z, y, xh, c))
SAME_CORE = [[y * 4 + xh * 2 + c for y in range(NY) for xh in range(NH)] for c in range(2)]
CORES = [[y * 4 + xh * 2 + c for c in range(2)] for y in range(NY) for xh in range(NH)]


def limit(mib):
    return pltpu.CompilerParams(vmem_limit_bytes=mib * 1024 * 1024)


def shift(x, pairs):
    return lax.ppermute(x, BOTH, pairs)


def pack_kernel(v_mask_ref, t_mask_ref, rows_ref, v_ref, t_ref, v_out, t_out, table_out):
    before = jnp.zeros_like(rows_ref[pl.ds(0, 1), :])
    for a in range(ABT_DEV):
        row = rows_ref[pl.ds(a, 1), :]
        table_out[pl.ds(a, 1), :] = before * row
        table_out[pl.ds(ABT_DEV + a, 1), :] = row
        before = before + row
    column = lax.axis_index("pair")
    flags = [v_mask_ref[a, column] for a in range(ABT_DEV)]
    chosen = sum(flags)
    taken = jnp.int32(0)
    for a in range(ABT_DEV):
        slot = jnp.where(flags[a] > 0, taken, chosen + a - taken)
        taken = taken + flags[a]

        @pl.when(slot < VCAP)
        def _():
            tile = v_ref[pl.ds(a * TILE, TILE), :] * flags[a].astype(jnp.bfloat16)
            v_out[pl.ds(pl.multiple_of(slot * TILE, TILE), TILE), :] = tile.T

    for p in range(t_mask_ref.shape[1]):
        for k in range(t_mask_ref.shape[0]):
            at = (pl.ds(p * TILE, TILE), pl.ds(k * TILE, TILE))
            tile = t_ref[at] * t_mask_ref[k, p].astype(jnp.bfloat16)
            for i in range(t_out.shape[0]):
                t_out[(i, *at)] = tile


def pack(v_ints, t_amps, v_mask, t_mask, copies):
    spread = (copies, *t_amps.shape)

    def block(shape):
        return pl.BlockSpec(shape, lambda i: (0,) * len(shape))

    return pl.pallas_call(
        pack_kernel,
        grid=(1,),
        out_shape=[
            jax.ShapeDtypeStruct((CHUNK, TILE), jnp.bfloat16),
            jax.ShapeDtypeStruct(spread, jnp.bfloat16),
            jax.ShapeDtypeStruct((2 * v_mask.shape[0], v_mask.shape[1]), jnp.int32),
        ],
        in_specs=[
            pl.BlockSpec(memory_space=pltpu.SMEM),
            pl.BlockSpec(memory_space=pltpu.SMEM),
            block(v_mask.shape),
            block(v_ints.shape),
            block(t_amps.shape),
        ],
        out_specs=[
            block((CHUNK, TILE)),
            block(spread),
            block((2 * v_mask.shape[0], v_mask.shape[1])),
        ],
        name="pack",
    )(v_mask, t_mask.T, v_mask, v_ints, t_amps)


def collect_kernel(pieces, count, *refs):
    core = lax.axis_index("virt") % 2
    to = 0
    for array, base, rows, side in pieces:
        refs[count][pl.ds(to, rows), :] = refs[array][pl.ds(start(base, side, core), rows), :]
        to += rows


def start(base, side, core):
    if side == STILL:
        return base
    return pl.multiple_of(base + (core if side == MINE else 1 - core) * CHUNK, CHUNK)


def indexed(pieces):
    arrays, where = [], []
    for array, *rest in pieces:
        at = next((i for i, seen in enumerate(arrays) if seen is array), len(arrays))
        if at == len(arrays):
            arrays.append(array)
        where.append((at, *rest))
    return arrays, where


def collect(*pieces):
    arrays, where = indexed(pieces)
    whole = pl.BlockSpec(memory_space=pltpu.VMEM)
    return pl.pallas_call(
        functools.partial(collect_kernel, where, len(arrays)),
        out_shape=jax.ShapeDtypeStruct((sum(p[2] for p in where), TILE), jnp.bfloat16),
        in_specs=[whole] * len(arrays),
        out_specs=whole,
        compiler_params=limit(4),
        name="collect",
    )(*arrays)


def product_kernel(plan, count, adds, last, table_ref, own_ref, other_ref, *refs):
    arrays, refs = refs[:count], refs[count:]
    before = None
    if adds:
        before, refs = refs[0], refs[1:]
    out_ref, left, right, table, sem = refs[:5]
    load = pltpu.make_async_copy(table_ref, table, sem)
    load.start()
    pair, virt = lax.axis_index("pair"), lax.axis_index("virt")
    xl, z, core = pair // NZ, pair % NZ, virt % 2
    way = 1 - 2 * core

    def column(across, step):
        return (xl if not across else 1 - xl) * NZ + lax.rem(z + step * way + NZ, NZ)

    for i, (_, _, _, across, step) in enumerate(plan):
        k = column(across, step)
        member = k // 4
        half = pl.multiple_of((k % 2) * TILE, TILE)
        mine = ((k // 2) % 2) == core
        left[:, pl.ds(i * TILE, TILE)] = jnp.where(
            mine, own_ref[member, :, pl.ds(half, TILE)], other_ref[member, :, pl.ds(half, TILE)]
        )
    load.wait()
    for i, (array, base, side, across, step) in enumerate(plan):
        k = column(across, step)
        first = start(base, side, core)
        for a in range(ABT_DEV):
            tile = arrays[array][pl.ds(pl.multiple_of(first + table[a, k] * TILE, TILE), TILE), :]
            flag = table[ABT_DEV + a, k].astype(jnp.bfloat16)
            right[pl.ds(i * TILE, TILE), pl.ds(a * TILE, TILE)] = tile * flag
    sends = []
    for i in range(ABT_DEV * TILE // 256):
        at = pl.ds(i * 256, 256)
        total = jnp.dot(left[...], right[:, at], preferred_element_type=jnp.float32)
        if before is not None:
            total = total + before[:, at]
        if not last:
            out_ref[:, at] = total
            continue
        stage, sems = refs[5:]
        stage[:, at] = total.astype(stage.dtype)
        sends.append(pltpu.make_async_copy(stage.at[:, at], out_ref.at[:, at], sems.at[i]))
        sends[-1].start()
    for send in sends:
        send.wait()


def product(table, t_own, t_other, chunks, before, last):
    rows, cols = t_own.shape[1], ABT_DEV * TILE
    arrays, plan = indexed(chunks)
    depth = len(plan) * TILE

    def kernel(*refs):
        product_kernel(plan, len(arrays), before is not None, last, *refs)

    whole, anywhere = pl.BlockSpec(memory_space=pltpu.VMEM), pl.BlockSpec(memory_space=pl.ANY)
    args = [table, t_own, t_other, *arrays] + ([] if before is None else [before])
    scratch = [
        pltpu.VMEM((rows, depth), jnp.bfloat16),
        pltpu.VMEM((depth, cols), jnp.bfloat16),
        pltpu.SMEM(table.shape, jnp.int32),
        pltpu.SemaphoreType.DMA,
    ]
    if last:
        scratch += [pltpu.VMEM((rows, cols), jnp.bfloat16), pltpu.SemaphoreType.DMA((cols // 256,))]
    return pl.pallas_call(
        kernel,
        out_shape=jax.ShapeDtypeStruct((rows, cols), jnp.bfloat16 if last else jnp.float32),
        in_specs=[anywhere] + [whole] * (len(args) - 1),
        out_specs=anywhere if last else whole,
        scratch_shapes=scratch,
        compiler_params=limit(14),
        cost_estimate=pl.CostEstimate(
            flops=2 * rows * depth * cols,
            bytes_accessed=4 * rows * cols + 2 * depth * TILE * 4,
            transcendentals=0,
        ),
    )(*args)


def both_cores(x):
    return lax.all_gather(x, "virt", axis=0, axis_index_groups=CORES, tiled=True)


def ladder(t_amps, v_ints, t_mask, v_mask):
    own, t_masked, table = pack(v_ints, t_amps, v_mask, t_mask, len(SAME_CORE[0]))
    side = shift(own, SIDE)
    d = {0: both_cores(own)}
    for s in range(1, 8):
        d[s] = shift(d[s - 1], RING)
    d8 = collect((d[3], 0, CHUNK, MINE))
    d8 = shift(d8, LEAP)
    t_own = lax.all_to_all(t_masked, "virt", 0, 0, axis_index_groups=SAME_CORE, tiled=True)
    t_other = shift(t_own, CORE)

    x = {}
    for parts in FORWARD.values():
        arrays = [(d8, 0, CHUNK, STILL) if s == 8 else (d[s], 0, 2 * CHUNK, STILL) for s in parts]
        packed = arrays[0][0]
        if len(arrays) > 1:
            packed = collect(*arrays)
        packed = shift(packed, SIDE)
        for i, s in enumerate(parts):
            x[s] = (packed, 2 * CHUNK * i)

    def exchange(columns):
        sources = [(x[s] if across else (d[s], 0)) for s, across in columns]
        rest = collect(*((array, base, CHUNK, OTHER) for array, base in sources))
        rest = shift(rest, CORE)
        return [(rest, i * CHUNK, STILL, across, s) for i, (s, across) in enumerate(columns)]

    def direct(*columns):
        return [
            (*(x[s] if across else (d[s], 0)), MINE, across, -s) for s, across in columns
        ]

    near = exchange([(s, False) for s in range(1, 7)] + [(s, True) for s in range(1, 5)])
    end = exchange([(5, True), (6, True), (7, False), (7, True)])
    zero = [(own, 0, STILL, False, 0), (side, 0, STILL, True, 0)]
    zero += direct(*((s, False) for s in range(1, 5)), (1, True), (2, True))
    first = direct(*((s, False) for s in range(5, 8)), *((s, True) for s in range(3, 7)))
    first += [(d8, 0, STILL, False, -8), (*x[8], STILL, True, -8)]
    second = near + direct((7, True))
    calls = (("zero", zero), ("first", first), ("second", second), ("third", end))
    total = None
    for name, chunks in calls:
        total = product(table, t_own, t_other, chunks, total, name == "third")
    return total


FORWARD = {"x12": (1, 2), "x34": (3, 4), "x58": (5, 8), "x6": (6,), "x7": (7,)}


def solution(mesh):
    return jax.shard_map(
        ladder,
        mesh=mesh,
        in_specs=(P("pair", "virt"), P("virt", "pair"), P("pair", "virt"), P("virt", None)),
        out_specs=P("pair", "virt"),
        check_vma=False,
    )
```
